32 devices in a mesh: grp: 2 (over y), leaf: 16 (over z, x, core).
Axes of the slice: x: 2, y: 2, z: 4, core: 2. Of those that a mesh axis runs over, the one named last changes fastest.
Arguments:
- vectors: float32 [16, 32768], P(None, ('grp', 'leaf')), may hold values from -6 to 6
- points: float32 [3, 32768], P(None, ('grp', 'leaf')), may hold values from -1 to 2
- near_lists: int32 [64, 6], P(('grp', 'leaf')), may hold values from -1 to 5, as said below
- inter_lists: int32 [64, 16], P(('grp', 'leaf')), may hold values from 0 to 31, as said below
- skeleton: int32 [64, 64], P(('grp', 'leaf')), may hold values from 0 to 511, as said below
- interp: float32 [64, 64, 512], P(('grp', 'leaf')), may hold values from -0.25 to 0.25
- transfer: float32 [64, 64, 128], P(('grp', 'leaf')), may hold values from -0.125 to 0.125
- coarse_points: float32 [2, 3, 128], replicated, may hold values from 0 to 1
Outputs:
- filtered: float32 [16, 32768], P(None, ('grp', 'leaf'))
The draws below stay inside these ranges and needn't reach their ends.
Inputs may be any that keep to these rules, and one draw needn't show every extreme that they name: `near_lists`: place w of leaf l's window is leaf (l // 2 - 1) * 2 + w. Slot 0 holds the leaf itself (2 + l % 2); the next slots hold distinct places of other leaves of the same subtree; then -1 to the end of the row. `inter_lists`: distinct leaves of the leaf's own subtree, numbered from the subtree's first leaf, none in the leaf's window. `skeleton`: distinct places within the leaf.
All inputs are finite; a program needn't handle non-finite values.
Results may differ from the reference program's by a relative error of at most 0.00013.
Values sent between devices are 32-bit elements; how exact they have to be, the bound alone decides.
No kernel may reach another device: no remote copies, remote signals or barrier semaphores. Data moves between devices by JAX's collectives and lax.ppermute only.
A program may use at most 64 MiB of HBM per device.

```python
import math
import jax
import jax.numpy as jnp
from jax import lax

P_SIZE = 512
R = 64
RC = 128
VEC = 16
NB = 6
ILEN = 16
LEAF_DEV = 2
LEAVES_SUB = 32
LEAVES = 64
POINTS = 32768
GROUPS = 2


def draw_points(key, part):
    leaf_ids = jnp.arange(LEAVES, dtype=jnp.int32)

    def spread(offset):
        result = jnp.zeros((LEAVES,), jnp.int32)
        for bit_pos in range(11):
            result = result + ((leaf_ids >> 3 * bit_pos + offset & 1) << bit_pos)
        return result.astype(jnp.float32)
    centres = jnp.stack([spread(0), spread(1), spread(2)]) * 0.08
    key_size, key_offset = jax.random.split(key)
    sizes = jnp.exp(jax.random.uniform(key_size, (LEAVES,), jnp.float32, math.log(1.5), math.log(3.0)))
    offsets = jax.random.uniform(key_offset, (3, LEAVES, P_SIZE), jnp.float32, -1.0, 1.0)
    coords = centres[:, :, None] + 0.04 * sizes[None, :, None] * offsets
    return coords.reshape(3, POINTS).astype(jnp.float32)


def draw_near_lists(key, part):
    width = 3 * LEAF_DEV
    leaf_ids = jnp.arange(LEAVES, dtype=jnp.int32)
    in_subtree = leaf_ids % LEAVES_SUB
    dev_place = in_subtree // LEAF_DEV
    own_place = in_subtree % LEAF_DEV
    places = jnp.arange(width, dtype=jnp.int32)
    target = (dev_place[:, None] - 1) * LEAF_DEV + places[None, :]
    usable = (target >= 0) & (target < LEAVES_SUB) & (places[None, :] != LEAF_DEV + own_place[:, None])
    key_score, key_dense, key_light = jax.random.split(key, 3)
    scores = jax.random.randint(key_score, (LEAVES, width), 0, 1 << 16) * (4 * width) + places[None, :]
    scores = scores + jnp.where(usable, 0, 1 << 28)
    order = jnp.argsort(scores, axis=1, stable=True)[:, :NB - 1].astype(jnp.int32)
    usable_count = jnp.sum(usable.astype(jnp.int32), axis=1)
    dense = jax.random.randint(key_dense, (LEAVES // LEAF_DEV,), 0, 4) == 0
    light = jax.random.randint(key_light, (LEAVES,), 0, NB // 2 + 1)
    others = jnp.where(dense[leaf_ids // LEAF_DEV], NB - 1, light)
    others = jnp.where(in_subtree == LEAF_DEV, NB - 1, others)
    others = jnp.minimum(others, usable_count)
    slots = jnp.arange(NB - 1, dtype=jnp.int32)
    rest = jnp.where(slots[None, :] < others[:, None], order, -1)
    return jnp.concatenate([(LEAF_DEV + own_place)[:, None], rest], axis=1).astype(jnp.int32)


def draw_inter_lists(key, part):
    leaf_ids = jnp.arange(LEAVES, dtype=jnp.int32)
    dev_place = leaf_ids % LEAVES_SUB // LEAF_DEV
    candidates = jnp.arange(LEAVES_SUB, dtype=jnp.int32)
    inside = (candidates[None, :] >= (dev_place[:, None] - 1) * LEAF_DEV) & (candidates[None, :] < (dev_place[:, None] + 2) * LEAF_DEV)
    scores = jax.random.randint(key, (LEAVES, LEAVES_SUB), 0, 1 << 16) * LEAVES_SUB + candidates[None, :]
    scores = scores + jnp.where(inside, 1 << 28, 0)
    return jnp.argsort(scores, axis=1, stable=True)[:, :ILEN].astype(jnp.int32)


def draw_skeleton(key, part):
    places = jnp.arange(P_SIZE, dtype=jnp.int32)
    scores = jax.random.randint(key, (LEAVES, P_SIZE), 0, 1 << 16) * P_SIZE + places[None, :]
    return jnp.argsort(scores, axis=1, stable=True)[:, :R].astype(jnp.int32)


def shard_levels(own_key, shape, shards, least, high):
    gain = 1.0
    for dim, parts in shards:
        steps = jax.random.uniform(jax.random.fold_in(jax.random.fold_in(own_key, 6), dim), (parts,), jnp.float32, least / len(shards), high / len(shards))
        gain = gain * jnp.repeat(jnp.exp(steps), shape[dim] // parts).reshape((-1,) + (1,) * (len(shape) - 1 - dim))
    return gain


def normal_values(own_key, extent, deviation, most, cuts=(), held_as=jnp.bfloat16):
    factor_of = shard_levels(own_key, extent, cuts, -0.22, 0.18) if cuts else 1.0
    array = jax.random.normal(own_key, extent, jnp.float32) * deviation * factor_of
    return jnp.minimum(jnp.maximum(array, -most), most).astype(held_as)


def setup_inputs(seed: int = 0) -> dict:
    arg_keys = jax.random.split(jax.random.key(seed), 9)
    return {
        "vectors": normal_values(arg_keys[0], (VEC, POINTS), 1.0, 6.0, ((1, 32),), jnp.float32),
        "points": draw_points(jax.random.fold_in(arg_keys[8], 71), 0),
        "near_lists": draw_near_lists(jax.random.fold_in(arg_keys[8], 71), 0),
        "inter_lists": draw_inter_lists(jax.random.fold_in(arg_keys[8], 71), 0),
        "skeleton": draw_skeleton(jax.random.fold_in(arg_keys[8], 71), 0),
        "interp": normal_values(arg_keys[5], (LEAVES, R, P_SIZE), P_SIZE ** -0.5, 0.25, ((0, 32),), jnp.float32),
        "transfer": normal_values(arg_keys[6], (LEAVES, R, RC), (32 * R) ** -0.5, 0.125, ((0, 32),), jnp.float32),
        "coarse_points": jnp.clip(jax.random.uniform(arg_keys[7], (GROUPS, 3, RC), jnp.float32, 0.0, 1.0), 0.0, 1.0),
    }


kappa_scale = 3.4641016151377544
centre = 0.05
half_width = 0.05
highest = lax.Precision.HIGHEST

def matern(source, target):
    delta_x = source[..., 0, :, None] - target[..., 0, None, :]
    delta_y = source[..., 1, :, None] - target[..., 1, None, :]
    delta_z = source[..., 2, :, None] - target[..., 2, None, :]
    scaled = kappa_scale * jnp.sqrt(delta_x * delta_x + delta_y * delta_y + delta_z * delta_z)
    return (1.0 + scaled) * jnp.exp(-scaled)

def operate(field, leaf_points, near_lists, inter_lists, skeleton, interp, transfer, coarse_points):
    leaf_vecs = field.reshape(VEC, LEAVES, P_SIZE).transpose(1, 0, 2)
    leaf_ids = jnp.arange(LEAVES, dtype=jnp.int32)
    base_leaf = (leaf_ids // LEAF_DEV - 1) * LEAF_DEV
    is_valid = near_lists >= 0
    near_global = jnp.where(is_valid, base_leaf[:, None] + near_lists, leaf_ids[:, None]).astype(jnp.int32)

    def near_one(leaf_id):
        sources = near_global[leaf_id]
        kernel = matern(leaf_points[sources], leaf_points[leaf_id])
        kernel = kernel * is_valid[leaf_id].astype(jnp.float32)[:, None, None]
        return jnp.einsum('kvp,kpq->vq', leaf_vecs[sources], kernel, precision=highest)
    near_part = lax.map(near_one, leaf_ids)
    coeffs = jnp.einsum('lvp,lrp->lvr', leaf_vecs, interp, precision=highest)
    skel_points = jnp.take_along_axis(leaf_points, skeleton[:, None, :], axis=2)
    list_global = ((leaf_ids // LEAVES_SUB * LEAVES_SUB)[:, None] + inter_lists).astype(jnp.int32)

    def far_one(leaf_id):
        sources = list_global[leaf_id]
        kernel = matern(skel_points[sources], skel_points[leaf_id])
        return jnp.einsum('svr,srq->vq', coeffs[sources], kernel, precision=highest)
    leaf_far = lax.map(far_one, leaf_ids)
    upward = jnp.einsum('lvr,lrc->lvc', coeffs, transfer, precision=highest)
    group_coeffs = upward.reshape(GROUPS, LEAVES_SUB, VEC, RC).sum(axis=1)
    coupling = matern(coarse_points[:, None], coarse_points[None, :])
    apart = (jnp.arange(GROUPS)[:, None] != jnp.arange(GROUPS)[None, :]).astype(jnp.float32)
    coarse_field = jnp.einsum('avr,agrq->gvq', group_coeffs, coupling * apart[:, :, None, None], precision=highest)
    leaf_coarse = coarse_field[leaf_ids // LEAVES_SUB]
    downward = leaf_far + jnp.einsum('lvc,lrc->lvr', leaf_coarse, transfer, precision=highest)
    far_part = jnp.einsum('lvr,lrp->lvp', downward, interp, precision=highest)
    total = (near_part + far_part) / (P_SIZE * NB)
    return total.transpose(1, 0, 2).reshape(VEC, POINTS)

def reference(vectors, points, near_lists, inter_lists, skeleton, interp, transfer, coarse_points):
    leaf_points = points.reshape(3, LEAVES, P_SIZE).transpose(1, 0, 2)

    def apply_once(field):
        return operate(field, leaf_points, near_lists, inter_lists, skeleton, interp, transfer, coarse_points)
    term_one = (apply_once(vectors) - centre * vectors) / half_width
    term_two = 2.0 * (apply_once(term_one) - centre * term_one) / half_width - vectors
    term_three = 2.0 * (apply_once(term_two) - centre * term_two) / half_width - term_one
    squares = lax.optimization_barrier(jnp.sum(term_three * term_three, axis=1))
    return term_three / jnp.sqrt(squares / POINTS + 1e-06)[:, None]
```

```python
import jax
import jax.numpy as jnp
from jax import lax
from jax.experimental import pallas as pl
from jax.experimental.pallas import tpu as pltpu
from jax.sharding import PartitionSpec as P

kappa_scale = 3.4641016151377544
log2_e = 1.4426950408889634
centre = 0.05
half_width = 0.05
highest = lax.Precision.HIGHEST
f32 = jnp.float32
bf16 = jnp.bfloat16

VMEM = pl.BlockSpec(memory_space=pltpu.VMEM)
SMEM = pl.BlockSpec(memory_space=pltpu.SMEM)
POINT_ROWS = 8


def split(x):
    hi = x.astype(bf16)
    return hi, (x - hi.astype(f32)).astype(bf16)


def dot3(left, right_hi, right_lo):
    rows = left.shape[0]
    hi, lo = split(left)
    both = jnp.dot(jnp.concatenate([hi, lo], axis=0), right_hi, preferred_element_type=f32)
    return both[:rows] + both[rows:] + jnp.dot(hi, right_lo, preferred_element_type=f32)


def dot_nt(left, right):
    return lax.dot_general(
        left, right, (((1,), (1,)), ((), ())), precision=highest, preferred_element_type=f32
    )


def matern(columns, rows):
    square = None
    for column, row in zip(columns, rows, strict=True):
        delta = column - row
        square = delta * delta if square is None else square + delta * delta
    scaled = square * lax.rsqrt(jnp.maximum(square, 1e-30))
    return (1.0 + scaled) * jnp.exp2(scaled * -log2_e)


def call(kernel, out_shape, in_specs, scratch=(), flops=0, limit=24, **kw):
    return pl.pallas_call(
        kernel,
        out_shape=out_shape,
        in_specs=in_specs,
        out_specs=jax.tree.map(lambda _: VMEM, out_shape),
        scratch_shapes=scratch,
        compiler_params=pltpu.CompilerParams(vmem_limit_bytes=limit << 20),
        cost_estimate=pl.CostEstimate(flops=flops, bytes_accessed=1 << 20, transcendentals=0),
        **kw,
    )


def base_place(kind, odd, per_dev):
    if kind == "own":
        return per_dev
    right = odd == (0 if kind == "pair" else 1)
    return jnp.where(right, 2 * per_dev, 0)


def near_kernel(kind, first, sizes):
    per_dev, leaf_size, vec, slots = sizes

    def body(*refs):
        refs = list(refs)
        lists, meta = refs[:2]
        own = refs[2]
        source = own if kind == "own" else refs[3]
        refs = refs[3:] if kind == "own" else refs[4:]
        if first:
            if kind != "own":
                acc, out, k_hi, k_lo, cols = refs
            else:
                acc, (out, k_hi, k_lo, cols) = None, refs
        else:
            if kind != "own":
                k_hi, k_lo, acc, out = refs
            else:
                acc, (k_hi, k_lo, out) = None, refs
        base = base_place(kind, lax.rem(meta[0], 2), per_dev)
        out[...] = jnp.zeros_like(out) if acc is None else acc[...]
        for j in range(per_dev):
            here = slice(j * leaf_size, (j + 1) * leaf_size)
            if first:
                cols[...] = (source[vec : vec + POINT_ROWS, here] * kappa_scale).T
            hits = []
            for leaf in range(per_dev):
                hit = lists[leaf, 0] == base + j
                for slot in range(1, slots):
                    hit = jnp.logical_or(hit, lists[leaf, slot] == base + j)
                hits.append(hit)
            for leaf in range(per_dev):
                there = slice(leaf * leaf_size, (leaf + 1) * leaf_size)

                @pl.when(hits[leaf])
                def _():
                    if first:
                        rows = [
                            own[vec + d : vec + d + 1, there] * kappa_scale for d in range(3)
                        ]
                        step = 32

                        def chunk(i, _):
                            at = pl.ds(pl.multiple_of(i * step, step), step)
                            columns = [cols[at, d : d + 1] for d in range(3)]
                            hi, lo = split(matern(columns, rows))
                            k_hi[j, at, there] = hi
                            k_lo[j, at, there] = lo
                            return 0

                        lax.fori_loop(0, leaf_size // step, chunk, 0, unroll=2)
                    out[:, there] += dot3(source[:vec, here], k_hi[j, :, there], k_lo[j, :, there])

    return body


def send_parts(out, coeffs, upward, meta, groups, leaves):
    group = meta[1]
    for i in range(leaves):
        out[group * leaves + i, : coeffs.shape[0]] = coeffs
    for t in range(1, groups):
        other = lax.rem(group + t, groups)
        for i in range(leaves):
            out[other * leaves + i, : upward.shape[0]] = upward


def coefficients(field, interp, transfer):
    per_dev, _, leaf_size = interp.shape
    parts = [
        dot_nt(field[:, j * leaf_size : (j + 1) * leaf_size], interp[j]) for j in range(per_dev)
    ]
    coeffs = jnp.concatenate(parts, axis=1)
    upward = jnp.dot(coeffs, transfer[...], precision=highest, preferred_element_type=f32)
    return coeffs, upward


def on_device(vectors, points, near_lists, inter_lists, skeleton, interp, transfer, coarse_points):
    per_dev, slots = near_lists.shape
    rank, leaf_size = interp.shape[1:]
    coarse = transfer.shape[2]
    vec, width = vectors.shape
    leaves, groups = lax.axis_size("leaf"), lax.axis_size("grp")
    devices = leaves * groups
    cols = per_dev * rank
    assert cols == coarse
    leaf_index, group_index = lax.axis_index("leaf"), lax.axis_index("grp")
    meta = jnp.stack([leaf_index, group_index]).astype(jnp.int32)
    transfer = transfer.reshape(cols, coarse)
    inner = [(i, i ^ 1) for i in range(leaves)]
    outer = [(i, i + 1) for i in range(1, leaves - 1, 2)]
    outer = outer + [(j, i) for i, j in outer]
    exchange = lambda x: lax.all_to_all(x, ("grp", "leaf"), 0, 0, tiled=True)
    sizes = (per_dev, leaf_size, vec, slots)
    shape = jax.ShapeDtypeStruct
    near_shape = shape((vec, width), f32)
    k_shape = shape((per_dev, leaf_size, width), bf16)

    stacked = jnp.concatenate(
        [vectors, points, jnp.zeros((POINT_ROWS - 3, width), f32)], axis=0
    )
    pair_window = lax.ppermute(stacked, "leaf", inner)
    next_window = lax.ppermute(stacked, "leaf", outer)

    def start_body(meta, field, skel, interp, transfer, out):
        coeffs, upward = coefficients(field[:vec], interp, transfer)
        spots = []
        for j in range(per_dev):
            places = lax.broadcasted_iota(jnp.int32, (leaf_size, rank), 0)
            pick = (places == skel[j : j + 1, :]).astype(f32)
            spots.append(
                jnp.dot(
                    field[vec:, j * leaf_size : (j + 1) * leaf_size],
                    pick,
                    precision=highest,
                    preferred_element_type=f32,
                )
            )
        spot = jnp.concatenate(spots, axis=1)
        own = jnp.concatenate([coeffs, spot], axis=0)
        send_parts(out, own, upward, meta, groups, leaves)

    payload = call(
        start_body,
        shape((devices, vec + POINT_ROWS, cols), f32),
        [SMEM, VMEM, VMEM, VMEM, VMEM],
        flops=10**7,
    )(meta, stacked, skeleton, interp, transfer)
    received = exchange(payload)

    near, own_hi, own_lo = call(
        near_kernel("own", True, sizes),
        (near_shape, k_shape, k_shape),
        [SMEM, SMEM, VMEM],
        scratch=[pltpu.VMEM((leaf_size, POINT_ROWS), f32)],
        flops=10**10,
    )(near_lists, meta, stacked)

    def couple_body(meta, coarse_points, transfer, out_hi, out_lo):
        group = meta[1]
        mine = coarse_points[group] * kappa_scale
        rows = [mine[d : d + 1] for d in range(3)]
        for t in range(1, groups):
            far = (coarse_points[lax.rem(group + t, groups)] * kappa_scale).T
            kernel = matern([far[:, d : d + 1] for d in range(3)], rows)
            at = slice((t - 1) * coarse, t * coarse)
            out_hi[at], out_lo[at] = split(dot_nt(kernel, transfer[...]))

    couple_shape = shape(((groups - 1) * coarse, cols), bf16)
    padded_coarse = jnp.pad(coarse_points, ((0, 0), (0, POINT_ROWS - 3), (0, 0)))
    couple_hi, couple_lo = call(
        couple_body, (couple_shape, couple_shape), [SMEM, VMEM, VMEM], flops=10**8
    )(meta, padded_coarse, transfer)

    def near_first(kind, window, acc):
        return call(
            near_kernel(kind, True, sizes),
            (near_shape, k_shape, k_shape),
            [SMEM, SMEM, VMEM, VMEM, VMEM],
            scratch=[pltpu.VMEM((leaf_size, POINT_ROWS), f32)],
            flops=10**10,
        )(near_lists, meta, stacked, window, acc)

    near, pair_hi, pair_lo = near_first("pair", pair_window, near)
    near, next_hi, next_lo = near_first("next", next_window, near)

    def far_body(lists, meta, received, out_hi, out_lo, marks):
        group, leaf = meta[1], meta[0]
        mine = received[group * leaves + leaf][vec:] * kappa_scale
        rows = [mine[d : d + 1] for d in range(3)]
        for m in range(leaves * per_dev):
            for j in range(per_dev):
                marks[m, j] = 0.0
        for j in range(per_dev):
            for s in range(lists.shape[1]):
                marks[lists[j, s], j] = 1.0
        lane_leaf = lax.broadcasted_iota(jnp.int32, (1, cols), 1) // rank

        def block(i, _):
            spots = (received[group * leaves + i][vec:] * kappa_scale).T
            for h in range(per_dev):
                part = spots[h * rank : (h + 1) * rank]
                kernel = matern([part[:, d : d + 1] for d in range(3)], rows)
                mark = jnp.zeros((1, cols), f32)
                for j in range(per_dev):
                    mark = jnp.where(lane_leaf == j, marks[i * per_dev + h, j], mark)
                at = pl.ds(pl.multiple_of((i * per_dev + h) * rank, rank), rank)
                hi, lo = split(kernel * mark)
                out_hi[at] = hi
                out_lo[at] = lo
            return 0

        lax.fori_loop(0, leaves, block, 0)

    far_shape = shape((leaves * cols, cols), bf16)
    far_hi, far_lo = call(
        far_body,
        (far_shape, far_shape),
        [SMEM, SMEM, VMEM],
        scratch=[pltpu.SMEM((leaves * per_dev, per_dev), f32)],
        flops=10**9,
    )(inter_lists, meta, received)

    def post_body(step, meta, received, far_hi, far_lo, couple_hi, couple_lo, near, *rest):
        if step == 1:
            field, interp, transfer, out, send = rest
        elif step == 2:
            field, before, interp, transfer, out, send = rest
        else:
            field, before, interp, out, send = rest
        group = meta[1]
        coeffs = jnp.concatenate(
            [received[group * leaves + i, :vec] for i in range(leaves)], axis=1
        )
        down = dot3(coeffs, far_hi[...], far_lo[...])
        totals = []
        for t in range(1, groups):
            first = lax.rem(group + t, groups) * leaves
            parts = [received[first + i, :vec] for i in range(leaves)]
            while len(parts) > 1:
                parts = [sum(parts[i : i + 2]) for i in range(0, len(parts), 2)]
            totals.append(parts[0])
        if totals:
            down = down + dot3(jnp.concatenate(totals, axis=1), couple_hi[...], couple_lo[...])
        news = []
        for j in range(per_dev):
            here = slice(j * leaf_size, (j + 1) * leaf_size)
            far = jnp.dot(
                down[:, j * rank : (j + 1) * rank],
                interp[j],
                precision=highest,
                preferred_element_type=f32,
            )
            applied = (near[:, here] + far) * (1.0 / (leaf_size * slots))
            term = (applied - centre * field[:vec, here]) * (1.0 / half_width)
            if step > 1:
                term = 2.0 * term - before[:vec, here]
            out[:, here] = term
            news.append(term)
        if step < 3:
            coeffs, upward = coefficients(jnp.concatenate(news, axis=1), interp, transfer)
            send_parts(send, coeffs, upward, meta, groups, leaves)
        else:
            squares = None
            for term in news:
                part = jnp.sum(term * term, axis=1, keepdims=True)
                squares = part if squares is None else squares + part
            diagonal = lax.broadcasted_iota(jnp.int32, (vec, 128), 0) == lax.broadcasted_iota(
                jnp.int32, (vec, 128), 1
            )
            row = jnp.sum(jnp.where(diagonal, squares, 0.0), axis=0, keepdims=True)
            for i in range(devices):
                send[i] = row

    def post(step, received, near, *rest):
        send_shape = (devices, vec, cols) if step < 3 else (devices, 1, 128)
        return call(
            lambda *refs: post_body(step, *refs),
            (near_shape, shape(send_shape, f32)),
            [SMEM] + [VMEM] * (6 + len(rest)),
            flops=10**8,
        )(meta, received, far_hi, far_lo, couple_hi, couple_lo, near, *rest)

    def near_again(field):
        pair_field = lax.ppermute(field, "leaf", inner)
        next_field = lax.ppermute(field, "leaf", outer)
        near = call(
            near_kernel("own", False, sizes), near_shape, [SMEM, SMEM, VMEM, VMEM, VMEM],
            flops=10**9,
        )(near_lists, meta, field, own_hi, own_lo)
        for kind, window, hi, lo in (
            ("pair", pair_field, pair_hi, pair_lo),
            ("next", next_field, next_hi, next_lo),
        ):
            near = call(
                near_kernel(kind, False, sizes),
                near_shape,
                [SMEM, SMEM, VMEM, VMEM, VMEM, VMEM, VMEM],
                flops=10**9,
            )(near_lists, meta, field, window, hi, lo, near)
        return near

    term_one, payload = post(1, received, near, stacked, interp, transfer)
    received = exchange(payload)
    near = near_again(term_one)
    term_two, payload = post(2, received, near, term_one, stacked, interp, transfer)
    received = exchange(payload)
    near = near_again(term_two)
    term_three, payload = post(3, received, near, term_two, term_one, interp)
    received = exchange(payload)
    squares = jnp.sum(received, axis=(0, 1))[:vec]
    total_points = width * devices
    return term_three / jnp.sqrt(squares / total_points + 1e-06)[:, None]


def solution(mesh):
    placed = (
        P(None, ("grp", "leaf")),
        P(None, ("grp", "leaf")),
        P(("grp", "leaf"), None),
        P(("grp", "leaf"), None),
        P(("grp", "leaf"), None),
        P(("grp", "leaf"), None, None),
        P(("grp", "leaf"), None, None),
        P(),
    )
    return jax.shard_map(
        on_device, mesh=mesh, in_specs=placed, out_specs=P(None, ("grp", "leaf")), check_vma=False
    )
```

```python
import jax
import jax.numpy as jnp
from jax import lax
from jax.experimental import pallas as pl
from jax.experimental.pallas import tpu as pltpu
from jax.sharding import PartitionSpec as P

kappa_scale = 3.4641016151377544
log2_e = 1.4426950408889634
centre = 0.05
half_width = 0.05
highest = lax.Precision.HIGHEST
f32 = jnp.float32
bf16 = jnp.bfloat16

HBM = pl.BlockSpec(memory_space=pltpu.HBM)
VMEM = pl.BlockSpec(memory_space=pltpu.VMEM)
SMEM = pl.BlockSpec(memory_space=pltpu.SMEM)
SUB = 8
NEAR_LIMIT = 54000
START_LIMIT = 6000


def split(x):
    hi = x.astype(bf16)
    return hi, (x - hi.astype(f32)).astype(bf16)


def dot3(left, right_hi, right_lo):
    rows = left.shape[0]
    hi, lo = split(left)
    both = jnp.dot(jnp.concatenate([hi, lo], axis=0), right_hi, preferred_element_type=f32)
    return both[:rows] + both[rows:] + jnp.dot(hi, right_lo, preferred_element_type=f32)


def dot_nt(left, right):
    return lax.dot_general(
        left, right, (((1,), (1,)), ((), ())), precision=highest, preferred_element_type=f32
    )


def dot_full(left, right):
    return jnp.dot(left, right, precision=highest, preferred_element_type=f32)


def three_parts(x):
    first = x.astype(bf16).astype(f32)
    second = (x - first).astype(bf16).astype(f32)
    return first, second, x - first - second


def distance_factors(points):
    x, y, z = points
    n = x.shape[1]
    norm = x * x + y * y + z * z
    at = lax.broadcasted_iota(jnp.int32, (SUB, n), 0)

    def rows(values):
        out = jnp.zeros((SUB, n), f32)
        for i, value in enumerate(values):
            out = jnp.where(at == i, value, out)
        return three_parts(out)

    s1, s2, s3 = rows([x, y, z, norm, 1.0])
    t1, t2, t3 = rows([-2.0 * x, -2.0 * y, -2.0 * z, 1.0, norm])
    source = jnp.concatenate([s1, s1, s2, s1, s3, s2], axis=0)
    target = jnp.concatenate([t1, t2, t1, t3, t1, t2], axis=0)
    return source, target


def source_factors(points):
    return distance_factors(points)[0].T.astype(bf16)


def target_factors(points):
    return distance_factors(points)[1].astype(bf16)


def matern(source, target):
    square = jnp.maximum(jnp.dot(source, target, preferred_element_type=f32), 1e-30)
    scaled = square * lax.rsqrt(square)
    return (1.0 + scaled) * jnp.exp2(scaled * -log2_e)


def coordinates(points, origin):
    return [(points[d : d + 1] - origin[d : d + 1, :1]) * kappa_scale for d in range(3)]


class Copies:
    def __init__(self, sems):
        self.sems, self.used, self.open = sems, 0, {}

    def start(self, name, source, target):
        copy = pltpu.make_async_copy(source, target, self.sems.at[self.used])
        self.used += 1
        copy.start()
        self.open[name] = copy

    def wait(self, *names):
        for name in names:
            self.open.pop(name).wait()

    def finish(self):
        self.wait(*list(self.open))


def call(kernel, out_shape, in_specs, out_specs, scratch=(), flops=0, limit=60 * 1024):
    return pl.pallas_call(
        kernel,
        out_shape=out_shape,
        in_specs=in_specs,
        out_specs=out_specs,
        scratch_shapes=scratch,
        compiler_params=pltpu.CompilerParams(vmem_limit_bytes=limit << 10),
        cost_estimate=pl.CostEstimate(flops=flops, bytes_accessed=1 << 20, transcendentals=0),
    )


def on_device(vectors, points, near_lists, inter_lists, skeleton, interp, transfer, coarse_points):
    per_dev, slots = near_lists.shape
    listed = inter_lists.shape[1]
    rank, leaf_size = interp.shape[1:]
    coarse = transfer.shape[2]
    vec, width = vectors.shape
    leaves, groups = lax.axis_size("leaf"), lax.axis_size("grp")
    devices = leaves * groups
    cols = per_dev * rank
    assert cols == coarse
    transfer = transfer.reshape(cols, coarse)
    inner = [(i, i ^ 1) for i in range(leaves)]
    outer = [(i, i + 1) for i in range(1, leaves - 1, 2)]
    outer = outer + [(j, i) for i, j in outer]
    exchange = lambda x: lax.all_to_all(x, ("grp", "leaf"), 0, 0, tiled=True)
    shape = jax.ShapeDtypeStruct
    field_shape = shape((vec, width), f32)
    field_scratch = pltpu.VMEM((vec, width), f32)
    couple_rows = (groups - 1) * coarse
    far_rows = leaves * cols
    limit = max(6000, far_rows * 3 // 2)
    leaf_slice = lambda j: slice(j * leaf_size, (j + 1) * leaf_size)

    def whereabouts():
        return lax.axis_index("leaf"), lax.axis_index("grp")

    def hit(place, lists, kind, j, leaf):
        odd = lax.rem(place[0], 2)
        if kind == 0:
            spot = per_dev + j
        else:
            spot = jnp.where(odd == kind - 1, 2 * per_dev, 0) + j
        found = lists[leaf, 0] == spot
        for slot in range(1, slots):
            found = jnp.logical_or(found, lists[leaf, slot] == spot)
        return found

    def coefficients(field, interp, transfer):
        coeffs = jnp.concatenate(
            [dot_nt(field[:, leaf_slice(j)], interp[j]) for j in range(per_dev)], axis=1
        )
        return coeffs, dot_full(coeffs, transfer[...])

    def send_parts(copies, out, own, upward, group):
        for i in range(leaves):
            copies.start(("own", i), own, out.at[group * leaves + i])
        for t in range(1, groups):
            first = lax.rem(group + t, groups) * leaves
            for i in range(leaves):
                copies.start(("up", t, i), upward, out.at[first + i])

    stacked = jnp.concatenate([vectors, points, jnp.zeros((SUB - 3, width), f32)], axis=0)
    pair_window = lax.ppermute(stacked, "leaf", inner)
    next_window = lax.ppermute(stacked, "leaf", outer)

    def start_body(
        field_in, points_in, skel_in, interp_in, transfer_in, coarse_in, near_lists_in, inter_lists_in,
        out, interp, transfer, coarse_points, near_lists, inter_lists,
        field, points, skel, own, up, sems,
    ):
        copies = Copies(sems)
        copies.start("points", points_in, points)
        copies.start("skel", skel_in, skel)
        copies.start("field", field_in, field)
        copies.start("interp", interp_in, interp)
        copies.start("transfer", transfer_in, transfer)
        copies.start("coarse", coarse_in, coarse_points)
        copies.start("near_lists", near_lists_in, near_lists)
        copies.start("inter_lists", inter_lists_in, inter_lists)
        own[vec:] = jnp.zeros((SUB, cols), f32)
        up[vec:] = jnp.zeros((SUB, cols), f32)
        copies.wait("points", "skel")
        for j in range(per_dev):
            places = lax.broadcasted_iota(jnp.int32, (leaf_size, rank), 0)
            pick = (places == skel[j : j + 1, :]).astype(f32)
            own[vec : vec + 3, j * rank : (j + 1) * rank] = dot_full(points[:, leaf_slice(j)], pick)
        copies.wait("field", "interp", "transfer")
        coeffs, upward = coefficients(field, interp, transfer)
        own[:vec] = coeffs
        up[:vec] = upward
        send_parts(copies, out, own, up, whereabouts()[1])
        copies.finish()

    payload, interp, transfer, coarse_points, near_lists, inter_lists = call(
        start_body,
        (
            shape((devices, vec + SUB, cols), f32),
            shape(interp.shape, f32),
            shape(transfer.shape, f32),
            shape((3, groups, coarse), f32),
            shape(near_lists.shape, jnp.int32),
            shape(inter_lists.shape, jnp.int32),
        ),
        [HBM] * 8,
        (HBM,) + (VMEM,) * 5,
        scratch=[
            field_scratch,
            pltpu.VMEM((3, width), f32),
            pltpu.VMEM((per_dev, rank), jnp.int32),
            pltpu.VMEM((vec + SUB, cols), f32),
            pltpu.VMEM((vec + SUB, cols), f32),
            pltpu.SemaphoreType.DMA((8 + devices,)),
        ],
        flops=10**7,
        limit=START_LIMIT,
    )(
        *[
            pltpu.with_memory_space_constraint(x, pltpu.HBM)
            for x in (
                vectors, points, skeleton, interp, transfer, coarse_points.transpose(1, 0, 2),
                near_lists, inter_lists,
            )
        ]
    )
    entries = [
        (kind, j, leaf) for kind in range(3) for j in range(per_dev) for leaf in range(per_dev)
    ]
    blocks_shape = (3 * per_dev, per_dev, 2, leaf_size, leaf_size)
    couple_shape = (2, couple_rows, cols)

    def near_first_body(
        lists, own, pair, other, coarse_points, transfer,
        near, couple, blocks_out, blocks, sems,
    ):
        def out_copy(block, leaf):
            return pltpu.make_async_copy(
                blocks.at[block, leaf], blocks_out.at[block, leaf], sems.at[block * per_dev + leaf]
            )

        place = whereabouts()
        group = place[1]
        mine = coarse_points[:, group]
        coarse_origin = mine[:, :1]
        target = target_factors(coordinates(mine, coarse_origin))
        for t in range(1, groups):
            far = coarse_points[:, lax.rem(group + t, groups)]
            kernel = matern(source_factors(coordinates(far, coarse_origin)), target)
            at = slice((t - 1) * coarse, t * coarse)
            couple[0, at], couple[1, at] = split(dot_nt(kernel, transfer[...]))
        windows = (own, pair, other)
        origin = own[vec : vec + 3][:, :1]
        targets = [
            target_factors(coordinates(own[vec : vec + 3, leaf_slice(leaf)], origin))
            for leaf in range(per_dev)
        ]
        near[...] = jnp.zeros_like(near)
        hits = [hit(place, lists, *entry) for entry in entries]
        for (kind, j, leaf), found in zip(entries, hits, strict=True):
            window = windows[kind]
            if leaf == 0:
                factors = source_factors(
                    coordinates(window[vec : vec + 3, leaf_slice(j)], origin)
                )
            block = kind * per_dev + j

            @pl.when(found)
            def _():
                step = 64
                for i in range(leaf_size // step):
                    at = slice(i * step, (i + 1) * step)
                    hi, lo = split(matern(factors[at], targets[leaf]))
                    blocks[block, leaf, 0, at] = hi
                    blocks[block, leaf, 1, at] = lo
                out_copy(block, leaf).start()
                near[:, leaf_slice(leaf)] += dot3(
                    window[:vec, leaf_slice(j)], blocks[block, leaf, 0], blocks[block, leaf, 1]
                )

        for (kind, j, leaf), found in zip(entries, hits, strict=True):

            @pl.when(found)
            def _():
                out_copy(kind * per_dev + j, leaf).wait()

    def near_again(kinds, windows, blocks, before=()):
        chosen = [entry for entry in entries if entry[0] in kinds]
        base = kinds[0] * per_dev
        shape_here = (len(kinds) * per_dev, *blocks_shape[1:])

        def body(lists, *refs):
            windows = refs[: len(kinds)]
            acc = refs[len(kinds) : len(kinds) + len(before)]
            blocks_in, near, blocks, sems = refs[len(kinds) + len(before) :]

            def in_copy(block, leaf):
                return pltpu.make_async_copy(
                    blocks_in.at[base + block, leaf], blocks.at[block, leaf],
                    sems.at[block * per_dev + leaf],
                )

            place = whereabouts()
            hits = [hit(place, lists, *entry) for entry in chosen]
            for (kind, j, leaf), found in zip(chosen, hits, strict=True):

                @pl.when(found)
                def _():
                    in_copy(kind * per_dev + j - base, leaf).start()

            near[...] = acc[0][...] if acc else jnp.zeros_like(near)
            for (kind, j, leaf), found in zip(chosen, hits, strict=True):
                block = kind * per_dev + j - base

                @pl.when(found)
                def _():
                    in_copy(block, leaf).wait()
                    near[:, leaf_slice(leaf)] += dot3(
                        windows[kind - kinds[0]][:, leaf_slice(j)],
                        blocks[block, leaf, 0],
                        blocks[block, leaf, 1],
                    )

        return call(
            body,
            field_shape,
            [SMEM] + [VMEM] * (len(kinds) + len(before)) + [HBM],
            VMEM,
            scratch=[pltpu.VMEM(shape_here, bf16), pltpu.SemaphoreType.DMA((len(chosen),))],
            flops=10**8,
            limit=NEAR_LIMIT,
        )(near_lists, *windows, *before, blocks)

    near_scratch = [
        pltpu.VMEM(blocks_shape, bf16),
        pltpu.SemaphoreType.DMA((len(entries),)),
    ]

    def halo(field):
        pair = lax.ppermute(field, "leaf", inner)
        other = lax.ppermute(field, "leaf", outer)
        return pair, other

    def build_far(place, lists, received, origin, far):
        group, leaf = place[1], place[0]
        target = target_factors(coordinates(received[group * leaves + leaf, vec : vec + 3], origin))
        lane_leaf = lax.broadcasted_iota(jnp.int32, (leaves * per_dev, cols), 1) // rank
        row_leaf = lax.broadcasted_iota(jnp.int32, (leaves * per_dev, cols), 0)
        mark = jnp.zeros((leaves * per_dev, cols), f32)
        for j in range(per_dev):
            for s in range(listed):
                here = jnp.logical_and(row_leaf == lists[j, s], lane_leaf == j)
                mark = jnp.where(here, 1.0, mark)
        for i in range(leaves):
            spots = received[group * leaves + i, vec : vec + 3]
            kernel = matern(source_factors(coordinates(spots, origin)), target)
            for h in range(per_dev):
                m = i * per_dev + h
                at = slice(m * rank, (m + 1) * rank)
                hi, lo = split(kernel[h * rank : (h + 1) * rank] * mark[m : m + 1])
                far[0, at] = hi
                far[1, at] = lo

    far_shape = (2, far_rows, cols)

    def post_body(step, lists, received, couple, interp, near, field, *rest):
        rest = list(rest)
        far, before = (None, None) if step == 1 else rest[:2]
        rest = rest if step == 1 else rest[2:]
        transfer = rest.pop(0) if step < 3 else None
        out, send = rest[:2]
        place = whereabouts()
        group = place[1]
        if step == 1:
            far = rest[2]
            origin = received[group * leaves + place[0], vec : vec + 3][:, :1]
            build_far(place, lists, received, origin, far)
        coeffs = jnp.concatenate(
            [received[group * leaves + i, :vec] for i in range(leaves)], axis=1
        )
        totals = []
        for t in range(1, groups):
            first = lax.rem(group + t, groups) * leaves
            parts = [received[first + i, :vec] for i in range(leaves)]
            while len(parts) > 1:
                parts = [sum(parts[i : i + 2]) for i in range(0, len(parts), 2)]
            totals.append(parts[0])
        down = dot3(coeffs, far[0], far[1])
        if totals:
            down = down + dot3(jnp.concatenate(totals, axis=1), couple[0], couple[1])
        news = []
        for j in range(per_dev):
            here = leaf_slice(j)
            far_part = dot_full(down[:, j * rank : (j + 1) * rank], interp[j])
            applied = (near[:, here] + far_part) * (1.0 / (leaf_size * slots))
            term = (applied - centre * field[:vec, here]) * (1.0 / half_width)
            if step > 1:
                term = 2.0 * term - before[:vec, here]
            news.append(term)
            out[:, here] = term
        if step < 3:
            coeffs, upward = coefficients(jnp.concatenate(news, axis=1), interp, transfer)
            for i in range(leaves):
                send[group * leaves + i] = coeffs
            for t in range(1, groups):
                first = lax.rem(group + t, groups) * leaves
                for i in range(leaves):
                    send[first + i] = upward
        else:
            squares = None
            for term in news:
                part = jnp.sum(term * term, axis=1, keepdims=True)
                squares = part if squares is None else squares + part
            diagonal = lax.broadcasted_iota(jnp.int32, (vec, 128), 0) == lax.broadcasted_iota(
                jnp.int32, (vec, 128), 1
            )
            row = jnp.sum(jnp.where(diagonal, squares, 0.0), axis=0, keepdims=True)
            for i in range(devices):
                send[i] = row

    def post(step, received, near, field, *rest):
        send_shape = (devices, vec, cols) if step < 3 else (devices, 1, 128)
        outs = [field_shape, shape(send_shape, f32)]
        if step == 1:
            outs.append(shape(far_shape, bf16))
        args = [received, couple, interp, near, field, *rest]
        if step < 3:
            args.append(transfer)
        return call(
            lambda *refs: post_body(step, *refs),
            tuple(outs),
            [SMEM] + [VMEM] * len(args),
            (VMEM,) * len(outs),
            flops=10**7,
            limit=limit,
        )(inter_lists, *args)

    def again(field):
        pair, other = halo(field)
        near = near_again((0, 1), (field, pair), blocks)
        return near_again((2,), (other,), blocks, (near,))

    received = exchange(payload)
    near, couple, blocks = call(
        near_first_body,
        (field_shape, shape(couple_shape, bf16), shape(blocks_shape, bf16)),
        [SMEM] + [VMEM] * 5,
        (VMEM, VMEM, HBM),
        scratch=near_scratch,
        flops=10**9,
        limit=NEAR_LIMIT,
    )(near_lists, stacked, pair_window, next_window, coarse_points, transfer)
    term_one, payload, far = post(1, received, near, stacked)
    received = exchange(payload)
    near = again(term_one)
    term_two, payload = post(2, received, near, term_one, far, stacked)
    received = exchange(payload)
    near = again(term_two)
    term_three, payload = post(3, received, near, term_two, far, term_one)
    received = exchange(payload)
    squares = jnp.sum(received, axis=(0, 1))[:vec]
    total_points = width * devices
    return term_three / jnp.sqrt(squares / total_points + 1e-06)[:, None]


def solution(mesh):
    placed = (
        P(None, ("grp", "leaf")),
        P(None, ("grp", "leaf")),
        P(("grp", "leaf"), None),
        P(("grp", "leaf"), None),
        P(("grp", "leaf"), None),
        P(("grp", "leaf"), None, None),
        P(("grp", "leaf"), None, None),
        P(),
    )

    return jax.shard_map(
        on_device, mesh=mesh, in_specs=placed, out_specs=P(None, ("grp", "leaf")), check_vma=False
    )
```

```python
import jax
import jax.numpy as jnp
from jax import lax
from jax.experimental import pallas as pl
from jax.experimental.pallas import tpu as pltpu
from jax.sharding import PartitionSpec as P

kappa_scale = 3.4641016151377544
log2_e = 1.4426950408889634
centre = 0.05
half_width = 0.05
highest = lax.Precision.HIGHEST
f32 = jnp.float32
bf16 = jnp.bfloat16

HBM = pl.BlockSpec(memory_space=pltpu.HBM)
VMEM = pl.BlockSpec(memory_space=pltpu.VMEM)
SMEM = pl.BlockSpec(memory_space=pltpu.SMEM)
SUB = 8
NEAR_LIMIT = 54000
START_LIMIT = 6000


def split(x):
    hi = x.astype(bf16)
    return hi, (x - hi.astype(f32)).astype(bf16)


def dot3(left, right_hi, right_lo):
    rows = left.shape[0]
    hi, lo = split(left)
    both = jnp.dot(jnp.concatenate([hi, lo], axis=0), right_hi, preferred_element_type=f32)
    return both[:rows] + both[rows:] + jnp.dot(hi, right_lo, preferred_element_type=f32)


def dot_nt(left, right):
    return lax.dot_general(
        left, right, (((1,), (1,)), ((), ())), precision=highest, preferred_element_type=f32
    )


def dot_full(left, right):
    return jnp.dot(left, right, precision=highest, preferred_element_type=f32)


def three_parts(x):
    first = x.astype(bf16).astype(f32)
    second = (x - first).astype(bf16).astype(f32)
    return first, second, x - first - second


def distance_factors(points):
    x, y, z = points
    n = x.shape[1]
    norm = x * x + y * y + z * z
    at = lax.broadcasted_iota(jnp.int32, (SUB, n), 0)

    def rows(values):
        out = jnp.zeros((SUB, n), f32)
        for i, value in enumerate(values):
            out = jnp.where(at == i, value, out)
        return three_parts(out)

    s1, s2, s3 = rows([x, y, z, norm, 1.0])
    t1, t2, t3 = rows([-2.0 * x, -2.0 * y, -2.0 * z, 1.0, norm])
    source = jnp.concatenate([s1, s1, s2, s1, s3, s2], axis=0)
    target = jnp.concatenate([t1, t2, t1, t3, t1, t2], axis=0)
    return source, target


def source_factors(points):
    return distance_factors(points)[0].T.astype(bf16)


def target_factors(points):
    return distance_factors(points)[1].astype(bf16)


def matern(source, target):
    square = jnp.maximum(jnp.dot(source, target, preferred_element_type=f32), 1e-30)
    scaled = square * lax.rsqrt(square)
    return (1.0 + scaled) * jnp.exp2(scaled * -log2_e)


def coordinates(points, origin):
    return [(points[d : d + 1] - origin[d : d + 1, :1]) * kappa_scale for d in range(3)]


class Copies:
    def __init__(self, sems):
        self.sems, self.used, self.open = sems, 0, {}

    def start(self, name, source, target):
        copy = pltpu.make_async_copy(source, target, self.sems.at[self.used])
        self.used += 1
        copy.start()
        self.open[name] = copy

    def wait(self, *names):
        for name in names:
            self.open.pop(name).wait()

    def finish(self):
        self.wait(*list(self.open))


def call(kernel, out_shape, in_specs, out_specs, scratch=(), flops=0, limit=60 * 1024):
    return pl.pallas_call(
        kernel,
        out_shape=out_shape,
        in_specs=in_specs,
        out_specs=out_specs,
        scratch_shapes=scratch,
        compiler_params=pltpu.CompilerParams(vmem_limit_bytes=limit << 10),
        cost_estimate=pl.CostEstimate(flops=flops, bytes_accessed=1 << 20, transcendentals=0),
    )


def on_device(vectors, points, near_lists, inter_lists, skeleton, interp, transfer, coarse_points):
    per_dev, slots = near_lists.shape
    listed = inter_lists.shape[1]
    rank, leaf_size = interp.shape[1:]
    coarse = transfer.shape[2]
    vec, width = vectors.shape
    leaves, groups = lax.axis_size("leaf"), lax.axis_size("grp")
    devices = leaves * groups
    cols = per_dev * rank
    assert cols == coarse
    transfer = transfer.reshape(cols, coarse)
    inner = [(i, i ^ 1) for i in range(leaves)]
    outer = [(i, i + 1) for i in range(1, leaves - 1, 2)]
    outer = outer + [(j, i) for i, j in outer]
    exchange = lambda x: lax.all_to_all(x, ("grp", "leaf"), 0, 0, tiled=True)
    shape = jax.ShapeDtypeStruct
    field_shape = shape((vec, width), f32)
    couple_rows = (groups - 1) * coarse
    far_rows = leaves * cols
    limit = max(6000, far_rows * 3 // 2)
    leaf_slice = lambda j: slice(j * leaf_size, (j + 1) * leaf_size)

    def whereabouts():
        return lax.axis_index("leaf"), lax.axis_index("grp")

    def hit(place, lists, kind, j, leaf):
        odd = lax.rem(place[0], 2)
        if kind == 0:
            spot = per_dev + j
        else:
            spot = jnp.where(odd == kind - 1, 2 * per_dev, 0) + j
        found = lists[leaf, 0] == spot
        for slot in range(1, slots):
            found = jnp.logical_or(found, lists[leaf, slot] == spot)
        return found

    def coefficients(field, interp, transfer):
        coeffs = jnp.concatenate(
            [dot_nt(field[:, leaf_slice(j)], interp[j]) for j in range(per_dev)], axis=1
        )
        return coeffs, dot_full(coeffs, transfer[...])

    def send_parts(copies, out, own, upward, group):
        for i in range(leaves):
            copies.start(("own", i), own, out.at[group * leaves + i])
        for t in range(1, groups):
            first = lax.rem(group + t, groups) * leaves
            for i in range(leaves):
                copies.start(("up", t, i), upward, out.at[first + i])

    def start_body(
        field_in, points_in, skel_in, interp_in, transfer_in, coarse_in, near_lists_in, inter_lists_in,
        out, stacked, interp, transfer, coarse_points, near_lists, inter_lists,
        points, skel, own, up, sems,
    ):
        field = stacked.at[pl.ds(0, vec)]
        copies = Copies(sems)
        copies.start("points", points_in, points)
        copies.start("skel", skel_in, skel)
        copies.start("field", field_in, field)
        copies.start("interp", interp_in, interp)
        copies.start("transfer", transfer_in, transfer)
        copies.start("coarse", coarse_in, coarse_points)
        copies.start("near_lists", near_lists_in, near_lists)
        copies.start("inter_lists", inter_lists_in, inter_lists)
        own[vec:] = jnp.zeros((SUB, cols), f32)
        up[vec:] = jnp.zeros((SUB, cols), f32)
        copies.wait("points", "skel")
        stacked[vec:] = jnp.zeros((SUB, width), f32)
        stacked[vec : vec + 3] = points[...]
        for j in range(per_dev):
            places = lax.broadcasted_iota(jnp.int32, (leaf_size, rank), 0)
            pick = (places == skel[j : j + 1, :]).astype(f32)
            own[vec : vec + 3, j * rank : (j + 1) * rank] = dot_full(points[:, leaf_slice(j)], pick)
        copies.wait("field", "interp", "transfer")
        coeffs, upward = coefficients(field, interp, transfer)
        own[:vec] = coeffs
        up[:vec] = upward
        send_parts(copies, out, own, up, whereabouts()[1])
        copies.finish()

    payload, stacked, interp, transfer, coarse_points, near_lists, inter_lists = call(
        start_body,
        (
            shape((devices, vec + SUB, cols), f32),
            shape((vec + SUB, width), f32),
            shape(interp.shape, f32),
            shape(transfer.shape, f32),
            shape((3, groups, coarse), f32),
            shape(near_lists.shape, jnp.int32),
            shape(inter_lists.shape, jnp.int32),
        ),
        [HBM] * 8,
        (HBM,) + (VMEM,) * 6,
        scratch=[
            pltpu.VMEM((3, width), f32),
            pltpu.VMEM((per_dev, rank), jnp.int32),
            pltpu.VMEM((vec + SUB, cols), f32),
            pltpu.VMEM((vec + SUB, cols), f32),
            pltpu.SemaphoreType.DMA((8 + devices,)),
        ],
        flops=10**7,
        limit=START_LIMIT,
    )(
        *[
            pltpu.with_memory_space_constraint(x, pltpu.HBM)
            for x in (
                vectors, points, skeleton, interp, transfer, coarse_points.transpose(1, 0, 2),
                near_lists, inter_lists,
            )
        ]
    )
    entries = [
        (kind, j, leaf) for kind in range(3) for j in range(per_dev) for leaf in range(per_dev)
    ]
    blocks_shape = (3 * per_dev, per_dev, 2, leaf_size, leaf_size)
    couple_shape = (2, couple_rows, cols)

    def near_first_body(
        lists, own, pair, other, coarse_points, transfer,
        near, blocks_out, couple,
        even, odd, factors, targets, fields, total, order, sems,
    ):
        place = whereabouts()
        origin = own[vec : vec + 3][:, :1]
        for leaf in range(per_dev):
            targets[leaf] = target_factors(coordinates(own[vec : vec + 3, leaf_slice(leaf)], origin))
            total[leaf] = jnp.zeros((vec, leaf_size), f32)
        count = jnp.int32(0)
        for i, (kind, j, leaf) in enumerate(entries):
            window = (own, pair, other)[kind]
            if leaf == 0:
                source = kind * per_dev + j
                factors[source] = source_factors(
                    coordinates(window[vec : vec + 3, leaf_slice(j)], origin)
                )
                fields[source] = jnp.concatenate(split(window[:vec, leaf_slice(j)]), axis=0)
            order[count] = i
            count = count + hit(place, lists, kind, j, leaf).astype(jnp.int32)

        def out_copy(i, buffer, side):
            entry = order[i]
            return pltpu.make_async_copy(
                buffer, blocks_out.at[entry // per_dev, lax.rem(entry, per_dev)], sems.at[side]
            )

        def make(i, buffer):
            entry = order[i]
            source, leaf = entry // per_dev, lax.rem(entry, per_dev)
            step = 64
            for c in range(leaf_size // step):
                at = slice(c * step, (c + 1) * step)
                hi, lo = split(matern(factors[source, at], targets[leaf]))
                buffer[0, at] = hi
                buffer[1, at] = lo

        def use(i, buffer):
            entry = order[i]
            source, leaf = entry // per_dev, lax.rem(entry, per_dev)
            field = fields[source]
            both = jnp.dot(field, buffer[0], preferred_element_type=f32)
            rest = jnp.dot(field[:vec], buffer[1], preferred_element_type=f32)
            total[leaf] += both[:vec] + both[vec:] + rest

        make(0, even)
        out_copy(0, even, 0).start()

        def turn(i, buffer, side, last):
            @pl.when(i >= 2)
            def _():
                out_copy(i - 2, buffer, side).wait()

            make(i, buffer)
            use(i - 1, last)
            out_copy(i, buffer, side).start()

        def two(t, _):
            turn(2 * t + 1, odd, 1, even)

            @pl.when(2 * t + 2 < count)
            def _():
                turn(2 * t + 2, even, 0, odd)

            return 0

        lax.fori_loop(0, count // 2, two, 0)
        ends_even = lax.rem(count, 2) == 1

        @pl.when(ends_even)
        def _():
            use(count - 1, even)

        @pl.when(jnp.logical_not(ends_even))
        def _():
            use(count - 1, odd)

        group = place[1]
        mine = coarse_points[:, group]
        coarse_origin = mine[:, :1]
        target = target_factors(coordinates(mine, coarse_origin))
        for t in range(1, groups):
            far = coarse_points[:, lax.rem(group + t, groups)]
            kernel = matern(source_factors(coordinates(far, coarse_origin)), target)
            at = slice((t - 1) * coarse, t * coarse)
            couple[0, at], couple[1, at] = split(dot_nt(kernel, transfer[...]))
        for leaf in range(per_dev):
            near[:, leaf_slice(leaf)] = total[leaf]
        last_even = jnp.where(ends_even, count - 1, count - 2)
        out_copy(last_even, even, 0).wait()

        @pl.when(count >= 2)
        def _():
            out_copy(jnp.where(ends_even, count - 2, count - 1), odd, 1).wait()

    def near_first(pair, other):
        block_shape = (2, leaf_size, leaf_size)
        return call(
            near_first_body,
            (field_shape, shape(blocks_shape, bf16), shape(couple_shape, bf16)),
            [SMEM] + [VMEM] * 5,
            (VMEM, HBM, VMEM),
            scratch=[
                pltpu.VMEM(block_shape, bf16),
                pltpu.VMEM(block_shape, bf16),
                pltpu.VMEM((3 * per_dev, leaf_size, 6 * SUB), bf16),
                pltpu.VMEM((per_dev, 6 * SUB, leaf_size), bf16),
                pltpu.VMEM((3 * per_dev, 2 * vec, leaf_size), bf16),
                pltpu.VMEM((per_dev, vec, leaf_size), f32),
                pltpu.SMEM((len(entries) + 1,), jnp.int32),
                pltpu.SemaphoreType.DMA((2,)),
            ],
            flops=10**9,
            limit=NEAR_LIMIT,
        )(near_lists, stacked, pair, other, coarse_points, transfer)

    def near_again(kinds, windows, blocks, before=()):
        chosen = [entry for entry in entries if entry[0] in kinds]
        base = kinds[0] * per_dev
        shape_here = (len(kinds) * per_dev, *blocks_shape[1:])

        def body(lists, *refs):
            windows = refs[: len(kinds)]
            acc = refs[len(kinds) : len(kinds) + len(before)]
            blocks_in, near, blocks, sems = refs[len(kinds) + len(before) :]

            def in_copy(block, leaf):
                return pltpu.make_async_copy(
                    blocks_in.at[base + block, leaf], blocks.at[block, leaf],
                    sems.at[block * per_dev + leaf],
                )

            place = whereabouts()
            hits = [hit(place, lists, *entry) for entry in chosen]
            for (kind, j, leaf), found in zip(chosen, hits, strict=True):

                @pl.when(found)
                def _():
                    in_copy(kind * per_dev + j - base, leaf).start()

            near[...] = acc[0][...] if acc else jnp.zeros_like(near)
            for (kind, j, leaf), found in zip(chosen, hits, strict=True):
                block = kind * per_dev + j - base

                @pl.when(found)
                def _():
                    in_copy(block, leaf).wait()
                    near[:, leaf_slice(leaf)] += dot3(
                        windows[kind - kinds[0]][:, leaf_slice(j)],
                        blocks[block, leaf, 0],
                        blocks[block, leaf, 1],
                    )

        return call(
            body,
            field_shape,
            [SMEM] + [VMEM] * (len(kinds) + len(before)) + [HBM],
            VMEM,
            scratch=[pltpu.VMEM(shape_here, bf16), pltpu.SemaphoreType.DMA((len(chosen),))],
            flops=10**8,
            limit=NEAR_LIMIT,
        )(near_lists, *windows, *before, pltpu.with_memory_space_constraint(blocks, pltpu.HBM))

    def halo(field):
        pair = lax.ppermute(field, "leaf", inner)
        other = lax.ppermute(field, "leaf", outer)
        return pair, other

    def build_far(place, lists, received, origin, far):
        group, leaf = place[1], place[0]
        target = target_factors(coordinates(received[group * leaves + leaf, vec : vec + 3], origin))
        lane_leaf = lax.broadcasted_iota(jnp.int32, (leaves * per_dev, cols), 1) // rank
        row_leaf = lax.broadcasted_iota(jnp.int32, (leaves * per_dev, cols), 0)
        mark = jnp.zeros((leaves * per_dev, cols), f32)
        for j in range(per_dev):
            for s in range(listed):
                here = jnp.logical_and(row_leaf == lists[j, s], lane_leaf == j)
                mark = jnp.where(here, 1.0, mark)
        for i in range(leaves):
            spots = received[group * leaves + i, vec : vec + 3]
            kernel = matern(source_factors(coordinates(spots, origin)), target)
            for h in range(per_dev):
                m = i * per_dev + h
                at = slice(m * rank, (m + 1) * rank)
                hi, lo = split(kernel[h * rank : (h + 1) * rank] * mark[m : m + 1])
                far[0, at] = hi
                far[1, at] = lo

    far_shape = (2, far_rows, cols)

    def post_body(step, lists, received, couple, interp, near, field, *rest):
        rest = list(rest)
        far, before = (None, None) if step == 1 else rest[:2]
        rest = rest if step == 1 else rest[2:]
        transfer = rest.pop(0) if step < 3 else None
        out, send = rest[:2]
        place = whereabouts()
        group = place[1]
        if step == 1:
            far = rest[2]
            origin = received[group * leaves + place[0], vec : vec + 3][:, :1]
            build_far(place, lists, received, origin, far)
        coeffs = jnp.concatenate(
            [received[group * leaves + i, :vec] for i in range(leaves)], axis=1
        )
        totals = []
        for t in range(1, groups):
            first = lax.rem(group + t, groups) * leaves
            parts = [received[first + i, :vec] for i in range(leaves)]
            while len(parts) > 1:
                parts = [sum(parts[i : i + 2]) for i in range(0, len(parts), 2)]
            totals.append(parts[0])
        down = dot3(coeffs, far[0], far[1])
        if totals:
            down = down + dot3(jnp.concatenate(totals, axis=1), couple[0], couple[1])
        news = []
        for j in range(per_dev):
            here = leaf_slice(j)
            far_part = dot_full(down[:, j * rank : (j + 1) * rank], interp[j])
            applied = (near[:, here] + far_part) * (1.0 / (leaf_size * slots))
            term = (applied - centre * field[:vec, here]) * (1.0 / half_width)
            if step > 1:
                term = 2.0 * term - before[:vec, here]
            news.append(term)
            out[:, here] = term
        if step < 3:
            coeffs, upward = coefficients(jnp.concatenate(news, axis=1), interp, transfer)
            for i in range(leaves):
                send[group * leaves + i] = coeffs
            for t in range(1, groups):
                first = lax.rem(group + t, groups) * leaves
                for i in range(leaves):
                    send[first + i] = upward
        else:
            squares = None
            for term in news:
                part = jnp.sum(term * term, axis=1, keepdims=True)
                squares = part if squares is None else squares + part
            diagonal = lax.broadcasted_iota(jnp.int32, (vec, 128), 0) == lax.broadcasted_iota(
                jnp.int32, (vec, 128), 1
            )
            row = jnp.sum(jnp.where(diagonal, squares, 0.0), axis=0, keepdims=True)
            for i in range(devices):
                send[i] = row

    def post(step, received, near, field, *rest):
        send_shape = (devices, vec, cols) if step < 3 else (devices, 1, 128)
        outs = [field_shape, shape(send_shape, f32)]
        if step == 1:
            outs.append(shape(far_shape, bf16))
        args = [received, couple, interp, near, field, *rest]
        if step < 3:
            args.append(transfer)
        return call(
            lambda *refs: post_body(step, *refs),
            tuple(outs),
            [SMEM] + [VMEM] * len(args),
            (VMEM,) * len(outs),
            flops=10**7,
            limit=limit,
        )(inter_lists, *args)

    received = exchange(payload)
    pair, other = halo(stacked)
    near, blocks, couple = near_first(pair, other)

    def again(field):
        pair, other = halo(field)
        near = near_again((0, 1), (field, pair), blocks)
        return near_again((2,), (other,), blocks, (near,))

    term_one, payload, far = post(1, received, near, stacked)
    received = exchange(payload)
    near = again(term_one)
    term_two, payload = post(2, received, near, term_one, far, stacked)
    received = exchange(payload)
    near = again(term_two)
    term_three, payload = post(3, received, near, term_two, far, term_one)
    received = exchange(payload)
    squares = jnp.sum(received, axis=(0, 1))[:vec]
    total_points = width * devices
    return term_three / jnp.sqrt(squares / total_points + 1e-06)[:, None]


def solution(mesh):
    placed = (
        P(None, ("grp", "leaf")),
        P(None, ("grp", "leaf")),
        P(("grp", "leaf"), None),
        P(("grp", "leaf"), None),
        P(("grp", "leaf"), None),
        P(("grp", "leaf"), None, None),
        P(("grp", "leaf"), None, None),
        P(),
    )

    return jax.shard_map(
        on_device, mesh=mesh, in_specs=placed, out_specs=P(None, ("grp", "leaf")), check_vma=False
    )
```

```python
import jax
import jax.numpy as jnp
from jax import lax
from jax.experimental import pallas as pl
from jax.experimental.pallas import tpu as pltpu
from jax.sharding import PartitionSpec as P

kappa_scale = 3.4641016151377544
log2_e = 1.4426950408889634
centre = 0.05
half_width = 0.05
f32 = jnp.float32
bf16 = jnp.bfloat16

HBM = pl.BlockSpec(memory_space=pltpu.HBM)
VMEM = pl.BlockSpec(memory_space=pltpu.VMEM)
SMEM = pl.BlockSpec(memory_space=pltpu.SMEM)
SUB = 8
NEAR_LIMIT = 54000
START_LIMIT = 6000


def split(x):
    hi = x.astype(bf16)
    return hi, (x - hi.astype(f32)).astype(bf16)


def dot3(left, right_hi, right_lo):
    rows = left.shape[0]
    hi, lo = split(left)
    both = jnp.dot(jnp.concatenate([hi, lo], axis=0), right_hi, preferred_element_type=f32)
    return both[:rows] + both[rows:] + jnp.dot(hi, right_lo, preferred_element_type=f32)


def dot3_nt(left, right_hi, right_lo):
    rows = left.shape[0]
    hi, lo = split(left)
    dot = lambda a, b: lax.dot_general(
        a, b, (((1,), (1,)), ((), ())), preferred_element_type=f32
    )
    both = dot(jnp.concatenate([hi, lo], axis=0), right_hi)
    return both[:rows] + both[rows:] + dot(hi, right_lo)


def three_parts(x):
    first = x.astype(bf16).astype(f32)
    second = (x - first).astype(bf16).astype(f32)
    return first, second, x - first - second


def distance_factors(points):
    x, y, z = points
    n = x.shape[1]
    norm = x * x + y * y + z * z
    at = lax.broadcasted_iota(jnp.int32, (SUB, n), 0)

    def rows(values):
        out = jnp.zeros((SUB, n), f32)
        for i, value in enumerate(values):
            out = jnp.where(at == i, value, out)
        return three_parts(out)

    s1, s2, s3 = rows([x, y, z, norm, 1.0])
    t1, t2, t3 = rows([-2.0 * x, -2.0 * y, -2.0 * z, 1.0, norm])
    source = jnp.concatenate([s1, s1, s2, s1, s3, s2], axis=0)
    target = jnp.concatenate([t1, t2, t1, t3, t1, t2], axis=0)
    return source, target


def source_factors(points):
    return distance_factors(points)[0].T.astype(bf16)


def target_factors(points):
    return distance_factors(points)[1].astype(bf16)


def matern(source, target):
    square = jnp.maximum(jnp.dot(source, target, preferred_element_type=f32), 1e-30)
    scaled = square * lax.rsqrt(square)
    return (1.0 + scaled) * jnp.exp2(scaled * -log2_e)


def coordinates(points, origin):
    return [(points[d : d + 1] - origin[d : d + 1, :1]) * kappa_scale for d in range(3)]


class Copies:
    def __init__(self, sems):
        self.sems, self.used, self.open = sems, 0, {}

    def start(self, name, source, target):
        copy = pltpu.make_async_copy(source, target, self.sems.at[self.used])
        self.used += 1
        copy.start()
        self.open[name] = copy

    def wait(self, *names):
        for name in names:
            self.open.pop(name).wait()

    def finish(self):
        self.wait(*list(self.open))


def call(kernel, out_shape, in_specs, out_specs, scratch=(), flops=0, limit=60 * 1024):
    return pl.pallas_call(
        kernel,
        out_shape=out_shape,
        in_specs=in_specs,
        out_specs=out_specs,
        scratch_shapes=scratch,
        compiler_params=pltpu.CompilerParams(vmem_limit_bytes=limit << 10),
        cost_estimate=pl.CostEstimate(flops=flops, bytes_accessed=1 << 20, transcendentals=0),
    )


def on_device(vectors, points, near_lists, inter_lists, skeleton, interp, transfer, coarse_points):
    per_dev, slots = near_lists.shape
    listed = inter_lists.shape[1]
    rank, leaf_size = interp.shape[1:]
    coarse = transfer.shape[2]
    vec, width = vectors.shape
    leaves, groups = lax.axis_size("leaf"), lax.axis_size("grp")
    devices = leaves * groups
    cols = per_dev * rank
    assert cols == coarse
    transfer = transfer.reshape(cols, coarse)
    inner = [(i, i ^ 1) for i in range(leaves)]
    outer = [(i, i + 1) for i in range(1, leaves - 1, 2)]
    outer = outer + [(j, i) for i, j in outer]
    exchange = lambda x: lax.all_to_all(x, ("grp", "leaf"), 0, 0, tiled=True)
    shape = jax.ShapeDtypeStruct
    field_shape = shape((vec, width), f32)
    couple_rows = (groups - 1) * coarse
    far_rows = leaves * cols
    limit = max(6000, far_rows * 3 // 2)
    leaf_slice = lambda j: slice(j * leaf_size, (j + 1) * leaf_size)

    def whereabouts():
        return lax.axis_index("leaf"), lax.axis_index("grp")

    def hit(place, lists, kind, j, leaf):
        odd = lax.rem(place[0], 2)
        if kind == 0:
            spot = per_dev + j
        else:
            spot = jnp.where(odd == kind - 1, 2 * per_dev, 0) + j
        found = lists[leaf, 0] == spot
        for slot in range(1, slots):
            found = jnp.logical_or(found, lists[leaf, slot] == spot)
        return found

    def coefficients(field, interp):
        return jnp.concatenate(
            [
                dot3_nt(field[:, leaf_slice(j)], interp[0, j], interp[1, j])
                for j in range(per_dev)
            ],
            axis=1,
        )

    def send_all(copies, out, own, up, coeffs, transfer, group):
        own[:vec] = coeffs
        for i in range(leaves):
            copies.start(("own", i), own, out.at[group * leaves + i])
        up[:vec] = dot3(coeffs, transfer[0], transfer[1])
        for t in range(1, groups):
            first = lax.rem(group + t, groups) * leaves
            for i in range(leaves):
                copies.start(("up", t, i), up, out.at[first + i])

    def start_body(
        field_in, points_in, skel_in, interp_in, transfer_in, coarse_in, near_lists_in, inter_lists_in,
        out, stacked, interp, transfer, coarse_points, near_lists, inter_lists,
        points, skel, whole_interp, whole_transfer, own, up, sems,
    ):
        field = stacked.at[pl.ds(0, vec)]
        copies = Copies(sems)
        copies.start("points", points_in, points)
        copies.start("skel", skel_in, skel)
        copies.start("field", field_in, field)
        copies.start("interp", interp_in, whole_interp)
        copies.start("transfer", transfer_in, whole_transfer)
        copies.start("coarse", coarse_in, coarse_points)
        copies.start("near_lists", near_lists_in, near_lists)
        copies.start("inter_lists", inter_lists_in, inter_lists)
        own[vec:] = jnp.zeros((SUB, cols), f32)
        up[vec:] = jnp.zeros((SUB, cols), f32)
        copies.wait("points", "skel")
        stacked[vec:] = jnp.zeros((SUB, width), f32)
        stacked[vec : vec + 3] = points[...]
        for j in range(per_dev):
            places = lax.broadcasted_iota(jnp.int32, (leaf_size, rank), 0)
            pick = (places == skel[j : j + 1, :]).astype(f32).astype(bf16)
            parts = jnp.concatenate(
                three_parts(stacked[vec:, leaf_slice(j)]), axis=0
            ).astype(bf16)
            spots = jnp.dot(parts, pick, preferred_element_type=f32)
            spots = spots[:SUB] + spots[SUB : 2 * SUB] + spots[2 * SUB :]
            own[vec:, j * rank : (j + 1) * rank] = spots
        copies.wait("interp", "field")
        for j in range(per_dev):
            interp[0, j], interp[1, j] = split(whole_interp[j])
        coeffs = coefficients(field, interp)
        copies.wait("transfer")
        transfer[0], transfer[1] = split(whole_transfer[...])
        send_all(copies, out, own, up, coeffs, transfer, whereabouts()[1])
        copies.finish()

    payload, stacked, interp, transfer, coarse_points, near_lists, inter_lists = call(
        start_body,
        (
            shape((devices, vec + SUB, cols), f32),
            shape((vec + SUB, width), f32),
            shape((2, *interp.shape), bf16),
            shape((2, *transfer.shape), bf16),
            shape((3, groups, coarse), f32),
            shape(near_lists.shape, jnp.int32),
            shape(inter_lists.shape, jnp.int32),
        ),
        [HBM] * 8,
        (HBM,) + (VMEM,) * 6,
        scratch=[
            pltpu.VMEM((3, width), f32),
            pltpu.VMEM((per_dev, rank), jnp.int32),
            pltpu.VMEM(interp.shape, f32),
            pltpu.VMEM(transfer.shape, f32),
            pltpu.VMEM((vec + SUB, cols), f32),
            pltpu.VMEM((vec + SUB, cols), f32),
            pltpu.SemaphoreType.DMA((8 + devices,)),
        ],
        flops=10**7,
        limit=START_LIMIT,
    )(
        *[
            pltpu.with_memory_space_constraint(x, pltpu.HBM)
            for x in (
                vectors, points, skeleton, interp, transfer, coarse_points.transpose(1, 0, 2),
                near_lists, inter_lists,
            )
        ]
    )
    entries = [
        (kind, j, leaf) for kind in range(3) for j in range(per_dev) for leaf in range(per_dev)
    ]
    blocks_shape = (3 * per_dev, per_dev, 2, leaf_size, leaf_size)
    couple_shape = (2, couple_rows, cols)

    def near_first_body(
        lists, own, pair, other, coarse_points, transfer,
        near, blocks_out, couple,
        even, odd, factors, targets, fields, total, order, sems,
    ):
        place = whereabouts()
        origin = own[vec : vec + 3][:, :1]
        for leaf in range(per_dev):
            targets[leaf] = target_factors(coordinates(own[vec : vec + 3, leaf_slice(leaf)], origin))
            total[leaf] = jnp.zeros((vec, leaf_size), f32)
        count = jnp.int32(0)
        for i, (kind, j, leaf) in enumerate(entries):
            window = (own, pair, other)[kind]
            if leaf == 0:
                source = kind * per_dev + j
                factors[source] = source_factors(
                    coordinates(window[vec : vec + 3, leaf_slice(j)], origin)
                )
                fields[source] = jnp.concatenate(split(window[:vec, leaf_slice(j)]), axis=0)
            order[count] = i
            count = count + hit(place, lists, kind, j, leaf).astype(jnp.int32)

        def out_copy(i, buffer, side):
            entry = order[i]
            return pltpu.make_async_copy(
                buffer, blocks_out.at[entry // per_dev, lax.rem(entry, per_dev)], sems.at[side]
            )

        def make(i, buffer):
            entry = order[i]
            source, leaf = entry // per_dev, lax.rem(entry, per_dev)
            step = 64
            for c in range(leaf_size // step):
                at = slice(c * step, (c + 1) * step)
                hi, lo = split(matern(factors[source, at], targets[leaf]))
                buffer[0, at] = hi
                buffer[1, at] = lo

        def use(i, buffer):
            entry = order[i]
            source, leaf = entry // per_dev, lax.rem(entry, per_dev)
            field = fields[source]
            both = jnp.dot(field, buffer[0], preferred_element_type=f32)
            rest = jnp.dot(field[:vec], buffer[1], preferred_element_type=f32)
            total[leaf] += both[:vec] + both[vec:] + rest

        make(0, even)
        out_copy(0, even, 0).start()

        def turn(i, buffer, side, last):
            @pl.when(i >= 2)
            def _():
                out_copy(i - 2, buffer, side).wait()

            make(i, buffer)
            use(i - 1, last)
            out_copy(i, buffer, side).start()

        def two(t, _):
            turn(2 * t + 1, odd, 1, even)

            @pl.when(2 * t + 2 < count)
            def _():
                turn(2 * t + 2, even, 0, odd)

            return 0

        lax.fori_loop(0, count // 2, two, 0)
        ends_even = lax.rem(count, 2) == 1

        @pl.when(ends_even)
        def _():
            use(count - 1, even)

        @pl.when(jnp.logical_not(ends_even))
        def _():
            use(count - 1, odd)

        group = place[1]
        mine = coarse_points[:, group]
        coarse_origin = mine[:, :1]
        target = target_factors(coordinates(mine, coarse_origin))
        for t in range(1, groups):
            far = coarse_points[:, lax.rem(group + t, groups)]
            kernel = matern(source_factors(coordinates(far, coarse_origin)), target)
            at = slice((t - 1) * coarse, t * coarse)
            couple[0, at], couple[1, at] = split(dot3_nt(kernel, transfer[0], transfer[1]))
        for leaf in range(per_dev):
            near[:, leaf_slice(leaf)] = total[leaf]
        last_even = jnp.where(ends_even, count - 1, count - 2)
        out_copy(last_even, even, 0).wait()

        @pl.when(count >= 2)
        def _():
            out_copy(jnp.where(ends_even, count - 2, count - 1), odd, 1).wait()

    def near_first(pair, other):
        block_shape = (2, leaf_size, leaf_size)
        return call(
            near_first_body,
            (field_shape, shape(blocks_shape, bf16), shape(couple_shape, bf16)),
            [SMEM] + [VMEM] * 5,
            (VMEM, HBM, VMEM),
            scratch=[
                pltpu.VMEM(block_shape, bf16),
                pltpu.VMEM(block_shape, bf16),
                pltpu.VMEM((3 * per_dev, leaf_size, 6 * SUB), bf16),
                pltpu.VMEM((per_dev, 6 * SUB, leaf_size), bf16),
                pltpu.VMEM((3 * per_dev, 2 * vec, leaf_size), bf16),
                pltpu.VMEM((per_dev, vec, leaf_size), f32),
                pltpu.SMEM((len(entries) + 1,), jnp.int32),
                pltpu.SemaphoreType.DMA((2,)),
            ],
            flops=10**9,
            limit=NEAR_LIMIT,
        )(near_lists, stacked, pair, other, coarse_points, transfer)

    def near_again(kinds, windows, blocks, before=()):
        chosen = [entry for entry in entries if entry[0] in kinds]
        base = kinds[0] * per_dev
        shape_here = (len(kinds) * per_dev, *blocks_shape[1:])

        def body(lists, *refs):
            windows = refs[: len(kinds)]
            acc = refs[len(kinds) : len(kinds) + len(before)]
            blocks_in, near, blocks, sems = refs[len(kinds) + len(before) :]

            def in_copy(block, leaf):
                return pltpu.make_async_copy(
                    blocks_in.at[base + block, leaf], blocks.at[block, leaf],
                    sems.at[block * per_dev + leaf],
                )

            place = whereabouts()
            hits = [hit(place, lists, *entry) for entry in chosen]
            for (kind, j, leaf), found in zip(chosen, hits, strict=True):

                @pl.when(found)
                def _():
                    in_copy(kind * per_dev + j - base, leaf).start()

            near[...] = acc[0][...] if acc else jnp.zeros_like(near)
            for (kind, j, leaf), found in zip(chosen, hits, strict=True):
                block = kind * per_dev + j - base

                @pl.when(found)
                def _():
                    in_copy(block, leaf).wait()
                    near[:, leaf_slice(leaf)] += dot3(
                        windows[kind - kinds[0]][:, leaf_slice(j)],
                        blocks[block, leaf, 0],
                        blocks[block, leaf, 1],
                    )

        return call(
            body,
            field_shape,
            [SMEM] + [VMEM] * (len(kinds) + len(before)) + [HBM],
            VMEM,
            scratch=[pltpu.VMEM(shape_here, bf16), pltpu.SemaphoreType.DMA((len(chosen),))],
            flops=10**8,
            limit=NEAR_LIMIT,
        )(near_lists, *windows, *before, pltpu.with_memory_space_constraint(blocks, pltpu.HBM))

    def halo(field):
        pair = lax.ppermute(field, "leaf", inner)
        other = lax.ppermute(field, "leaf", outer)
        return pair, other

    def build_far(place, lists, received, origin, far):
        group, leaf = place[1], place[0]
        target = target_factors(coordinates(received[group * leaves + leaf, vec : vec + 3], origin))
        lane_leaf = lax.broadcasted_iota(jnp.int32, (leaves * per_dev, cols), 1) // rank
        row_leaf = lax.broadcasted_iota(jnp.int32, (leaves * per_dev, cols), 0)
        mark = jnp.zeros((leaves * per_dev, cols), f32)
        for j in range(per_dev):
            for s in range(listed):
                here = jnp.logical_and(row_leaf == lists[j, s], lane_leaf == j)
                mark = jnp.where(here, 1.0, mark)
        for i in range(leaves):
            spots = received[group * leaves + i, vec : vec + 3]
            kernel = matern(source_factors(coordinates(spots, origin)), target)
            for h in range(per_dev):
                m = i * per_dev + h
                at = slice(m * rank, (m + 1) * rank)
                hi, lo = split(kernel[h * rank : (h + 1) * rank] * mark[m : m + 1])
                far[0, at] = hi
                far[1, at] = lo

    far_shape = (2, far_rows + couple_rows, cols)

    def post_body(step, *refs):
        refs = list(refs)
        lists, couple = (refs.pop(0), refs.pop(0)) if step == 1 else (None, None)
        received, interp, near, field = refs[:4]
        refs = refs[4:]
        far, before = (None, None) if step == 1 else (refs.pop(0), refs.pop(0))
        transfer = refs.pop(0) if step < 3 else None
        out, send = refs.pop(0), refs.pop(0)
        place = whereabouts()
        group = place[1]
        if step == 1:
            far = refs.pop(0)
            origin = received[group * leaves + place[0], vec : vec + 3][:, :1]
            build_far(place, lists, received, origin, far)
            far[:, far_rows:] = couple[...]
        parts = [received[group * leaves + i, :vec] for i in range(leaves)]
        for t in range(1, groups):
            first = lax.rem(group + t, groups) * leaves
            sums = [received[first + i, :vec] for i in range(leaves)]
            while len(sums) > 1:
                sums = [sum(sums[i : i + 2]) for i in range(0, len(sums), 2)]
            parts += sums
        down = dot3(jnp.concatenate(parts, axis=1), far[0], far[1])
        news = []
        for j in range(per_dev):
            here = leaf_slice(j)
            far_part = dot3(down[:, j * rank : (j + 1) * rank], interp[0, j], interp[1, j])
            applied = (near[:, here] + far_part) * (1.0 / (leaf_size * slots))
            term = (applied - centre * field[:vec, here]) * (1.0 / half_width)
            if step > 1:
                term = 2.0 * term - before[:vec, here]
            news.append(term)
            out[:, here] = term
        if step < 3:
            own, up, sems = refs
            copies = Copies(sems)
            coeffs = coefficients(jnp.concatenate(news, axis=1), interp)
            send_all(copies, send, own, up, coeffs, transfer, group)
            copies.finish()
        else:
            squares = None
            for term in news:
                part = jnp.sum(term * term, axis=1, keepdims=True)
                squares = part if squares is None else squares + part
            diagonal = lax.broadcasted_iota(jnp.int32, (vec, 128), 0) == lax.broadcasted_iota(
                jnp.int32, (vec, 128), 1
            )
            row = jnp.sum(jnp.where(diagonal, squares, 0.0), axis=0, keepdims=True)
            for i in range(devices):
                send[i] = row

    def post(step, received, near, field, *rest):
        send_shape = (devices, vec, cols) if step < 3 else (devices, 1, 128)
        outs = [field_shape, shape(send_shape, f32)]
        specs = [VMEM, HBM if step < 3 else VMEM]
        args = [received, interp, near, field, *rest]
        if step == 1:
            outs.append(shape(far_shape, bf16))
            specs.append(VMEM)
            args = [inter_lists, couple, *args]
        scratch = []
        if step < 3:
            args.append(transfer)
            scratch = [
                pltpu.VMEM((vec, cols), f32),
                pltpu.VMEM((vec, cols), f32),
                pltpu.SemaphoreType.DMA((devices,)),
            ]
        in_specs = [VMEM] * len(args)
        if step == 1:
            in_specs[0] = SMEM
        return call(
            lambda *refs: post_body(step, *refs),
            tuple(outs),
            in_specs,
            tuple(specs),
            scratch=scratch,
            flops=10**7,
            limit=limit,
        )(*args)

    received = exchange(payload)
    pair, other = halo(stacked)
    near, blocks, couple = near_first(pair, other)

    def again(field):
        pair, other = halo(field)
        near = near_again((0, 1), (field, pair), blocks)
        return near_again((2,), (other,), blocks, (near,))

    term_one, payload, far = post(1, received, near, stacked)
    received = exchange(payload)
    near = again(term_one)
    term_two, payload = post(2, received, near, term_one, far, stacked)
    received = exchange(payload)
    near = again(term_two)
    term_three, payload = post(3, received, near, term_two, far, term_one)
    received = exchange(payload)
    squares = jnp.sum(received, axis=(0, 1))[:vec]
    total_points = width * devices
    return term_three / jnp.sqrt(squares / total_points + 1e-06)[:, None]


def solution(mesh):
    placed = (
        P(None, ("grp", "leaf")),
        P(None, ("grp", "leaf")),
        P(("grp", "leaf"), None),
        P(("grp", "leaf"), None),
        P(("grp", "leaf"), None),
        P(("grp", "leaf"), None, None),
        P(("grp", "leaf"), None, None),
        P(),
    )

    return jax.shard_map(
        on_device, mesh=mesh, in_specs=placed, out_specs=P(None, ("grp", "leaf")), check_vma=False
    )
```

```python
import jax
import jax.numpy as jnp
from jax import lax
from jax.experimental import pallas as pl
from jax.experimental.pallas import tpu as pltpu
from jax.sharding import PartitionSpec as P

kappa_scale = 3.4641016151377544
log2_e = 1.4426950408889634
centre = 0.05
half_width = 0.05
f32 = jnp.float32
bf16 = jnp.bfloat16

HBM = pl.BlockSpec(memory_space=pltpu.HBM)
VMEM = pl.BlockSpec(memory_space=pltpu.VMEM)
SMEM = pl.BlockSpec(memory_space=pltpu.SMEM)
SUB = 8
NEAR_LIMIT = 54000
INNER_LIMIT = 16000
START_LIMIT = 6000


def split(x):
    hi = x.astype(bf16)
    return hi, (x - hi.astype(f32)).astype(bf16)


def dot3(left, right_hi, right_lo):
    rows = left.shape[0]
    hi, lo = split(left)
    both = jnp.dot(jnp.concatenate([hi, lo], axis=0), right_hi, preferred_element_type=f32)
    return both[:rows] + both[rows:] + jnp.dot(hi, right_lo, preferred_element_type=f32)


def dot3_nt(left, right_hi, right_lo):
    rows = left.shape[0]
    hi, lo = split(left)
    dot = lambda a, b: lax.dot_general(
        a, b, (((1,), (1,)), ((), ())), preferred_element_type=f32
    )
    both = dot(jnp.concatenate([hi, lo], axis=0), right_hi)
    return both[:rows] + both[rows:] + dot(hi, right_lo)


def three_parts(x):
    first = x.astype(bf16).astype(f32)
    second = (x - first).astype(bf16).astype(f32)
    return first, second, x - first - second


def distance_factors(points):
    x, y, z = points
    n = x.shape[1]
    norm = x * x + y * y + z * z
    at = lax.broadcasted_iota(jnp.int32, (SUB, n), 0)

    def rows(values):
        out = jnp.zeros((SUB, n), f32)
        for i, value in enumerate(values):
            out = jnp.where(at == i, value, out)
        return three_parts(out)

    s1, s2, s3 = rows([x, y, z, norm, 1.0])
    t1, t2, t3 = rows([-2.0 * x, -2.0 * y, -2.0 * z, 1.0, norm])
    source = jnp.concatenate([s1, s1, s2, s1, s3, s2], axis=0)
    target = jnp.concatenate([t1, t2, t1, t3, t1, t2], axis=0)
    return source, target


def source_factors(points):
    return distance_factors(points)[0].T.astype(bf16)


def target_factors(points):
    return distance_factors(points)[1].astype(bf16)


def matern(source, target):
    square = jnp.maximum(jnp.dot(source, target, preferred_element_type=f32), 1e-30)
    scaled = square * lax.rsqrt(square)
    return (1.0 + scaled) * jnp.exp2(scaled * -log2_e)


def coordinates(points, origin):
    return [(points[d : d + 1] - origin[d : d + 1, :1]) * kappa_scale for d in range(3)]


class Copies:
    def __init__(self, sems):
        self.sems, self.used, self.open = sems, 0, {}

    def start(self, name, source, target):
        copy = pltpu.make_async_copy(source, target, self.sems.at[self.used])
        self.used += 1
        copy.start()
        self.open[name] = copy

    def wait(self, *names):
        for name in names:
            self.open.pop(name).wait()

    def finish(self):
        self.wait(*list(self.open))


def call(kernel, out_shape, in_specs, out_specs, scratch=(), flops=0, limit=60 * 1024):
    return pl.pallas_call(
        kernel,
        out_shape=out_shape,
        in_specs=in_specs,
        out_specs=out_specs,
        scratch_shapes=scratch,
        compiler_params=pltpu.CompilerParams(vmem_limit_bytes=limit << 10),
        cost_estimate=pl.CostEstimate(flops=flops, bytes_accessed=1 << 20, transcendentals=0),
    )


def on_device(vectors, points, near_lists, inter_lists, skeleton, interp, transfer, coarse_points):
    per_dev, slots = near_lists.shape
    listed = inter_lists.shape[1]
    rank, leaf_size = interp.shape[1:]
    coarse = transfer.shape[2]
    vec, width = vectors.shape
    leaves, groups = lax.axis_size("leaf"), lax.axis_size("grp")
    devices = leaves * groups
    cols = per_dev * rank
    assert cols == coarse
    transfer = transfer.reshape(cols, coarse)
    inner = [(i, i ^ 1) for i in range(leaves)]
    outer = [(i, i + 1) for i in range(1, leaves - 1, 2)]
    outer = outer + [(j, i) for i, j in outer]
    exchange = lambda x: lax.all_to_all(x, ("grp", "leaf"), 0, 0, tiled=True)
    shape = jax.ShapeDtypeStruct
    field_shape = shape((vec, width), f32)
    couple_rows = (groups - 1) * coarse
    far_rows = leaves * cols
    limit = max(6000, far_rows * 3 // 2)
    leaf_slice = lambda j: slice(j * leaf_size, (j + 1) * leaf_size)

    def whereabouts():
        return lax.axis_index("leaf"), lax.axis_index("grp")

    def hit(place, lists, kind, j, leaf):
        odd = lax.rem(place[0], 2)
        if kind == 0:
            spot = per_dev + j
        else:
            spot = jnp.where(odd == kind - 1, 2 * per_dev, 0) + j
        found = lists[leaf, 0] == spot
        for slot in range(1, slots):
            found = jnp.logical_or(found, lists[leaf, slot] == spot)
        return found

    def coefficients(field, interp):
        return jnp.concatenate(
            [
                dot3_nt(field[:, leaf_slice(j)], interp[0, j], interp[1, j])
                for j in range(per_dev)
            ],
            axis=1,
        )

    def send_all(copies, out, own, up, coeffs, transfer, group):
        own[:vec] = coeffs
        for i in range(leaves):
            copies.start(("own", i), own, out.at[group * leaves + i])
        up[:vec] = dot3(coeffs, transfer[0], transfer[1])
        for t in range(1, groups):
            first = lax.rem(group + t, groups) * leaves
            for i in range(leaves):
                copies.start(("up", t, i), up, out.at[first + i])

    def start_body(
        field_in, points_in, skel_in, interp_in, transfer_in, coarse_in, near_lists_in, inter_lists_in,
        out, stacked, interp, transfer, coarse_points, near_lists, inter_lists,
        points, skel, whole_interp, whole_transfer, own, up, sems,
    ):
        field = stacked.at[pl.ds(0, vec)]
        copies = Copies(sems)
        copies.start("points", points_in, points)
        copies.start("skel", skel_in, skel)
        copies.start("field", field_in, field)
        copies.start("interp", interp_in, whole_interp)
        copies.start("transfer", transfer_in, whole_transfer)
        copies.start("coarse", coarse_in, coarse_points)
        copies.start("near_lists", near_lists_in, near_lists)
        copies.start("inter_lists", inter_lists_in, inter_lists)
        own[vec:] = jnp.zeros((SUB, cols), f32)
        up[vec:] = jnp.zeros((SUB, cols), f32)
        copies.wait("points", "skel")
        stacked[vec:] = jnp.zeros((SUB, width), f32)
        stacked[vec : vec + 3] = points[...]
        for j in range(per_dev):
            places = lax.broadcasted_iota(jnp.int32, (leaf_size, rank), 0)
            pick = (places == skel[j : j + 1, :]).astype(f32).astype(bf16)
            parts = jnp.concatenate(
                three_parts(stacked[vec:, leaf_slice(j)]), axis=0
            ).astype(bf16)
            spots = jnp.dot(parts, pick, preferred_element_type=f32)
            spots = spots[:SUB] + spots[SUB : 2 * SUB] + spots[2 * SUB :]
            own[vec:, j * rank : (j + 1) * rank] = spots
        copies.wait("interp", "field")
        for j in range(per_dev):
            interp[0, j], interp[1, j] = split(whole_interp[j])
        coeffs = coefficients(field, interp)
        copies.wait("transfer")
        transfer[0], transfer[1] = split(whole_transfer[...])
        send_all(copies, out, own, up, coeffs, transfer, whereabouts()[1])
        copies.finish()

    payload, stacked, interp, transfer, coarse_points, near_lists, inter_lists = call(
        start_body,
        (
            shape((devices, vec + SUB, cols), f32),
            shape((vec + SUB, width), f32),
            shape((2, *interp.shape), bf16),
            shape((2, *transfer.shape), bf16),
            shape((3, groups, coarse), f32),
            shape(near_lists.shape, jnp.int32),
            shape(inter_lists.shape, jnp.int32),
        ),
        [HBM] * 8,
        (HBM,) + (VMEM,) * 6,
        scratch=[
            pltpu.VMEM((3, width), f32),
            pltpu.VMEM((per_dev, rank), jnp.int32),
            pltpu.VMEM(interp.shape, f32),
            pltpu.VMEM(transfer.shape, f32),
            pltpu.VMEM((vec + SUB, cols), f32),
            pltpu.VMEM((vec + SUB, cols), f32),
            pltpu.SemaphoreType.DMA((8 + devices,)),
        ],
        flops=10**7,
        limit=START_LIMIT,
    )(
        *[
            pltpu.with_memory_space_constraint(x, pltpu.HBM)
            for x in (
                vectors, points, skeleton, interp, transfer, coarse_points.transpose(1, 0, 2),
                near_lists, inter_lists,
            )
        ]
    )
    entries = [
        (kind, j, leaf) for kind in range(3) for j in range(per_dev) for leaf in range(per_dev)
    ]
    blocks_shape = (3 * per_dev, per_dev, 2, leaf_size, leaf_size)
    couple_shape = (2, couple_rows, cols)

    def near_first_body(
        lists, own, pair, other, coarse_points, transfer,
        near, blocks_out, other_out, couple,
        even, odd, factors, targets, fields, total, order, sems,
    ):
        place = whereabouts()
        origin = own[vec : vec + 3][:, :1]
        for leaf in range(per_dev):
            targets[leaf] = target_factors(coordinates(own[vec : vec + 3, leaf_slice(leaf)], origin))
            total[leaf] = jnp.zeros((vec, leaf_size), f32)
        count = jnp.int32(0)
        for i, (kind, j, leaf) in enumerate(entries):
            window = (own, pair, other)[kind]
            if leaf == 0:
                source = kind * per_dev + j
                factors[source] = source_factors(
                    coordinates(window[vec : vec + 3, leaf_slice(j)], origin)
                )
                fields[source] = jnp.concatenate(split(window[:vec, leaf_slice(j)]), axis=0)
            order[count] = i
            count = count + hit(place, lists, kind, j, leaf).astype(jnp.int32)

        inner_entries = 2 * per_dev * per_dev

        def out_start(i, buffer, side):
            entry = order[i]
            source, leaf = entry // per_dev, lax.rem(entry, per_dev)

            @pl.when(entry < inner_entries)
            def _():
                pltpu.make_async_copy(buffer, blocks_out.at[source, leaf], sems.at[side]).start()

            @pl.when(entry >= inner_entries)
            def _():
                pltpu.make_async_copy(
                    buffer, other_out.at[source - 2 * per_dev, leaf], sems.at[side]
                ).start()

        def out_wait(i, buffer, side):
            entry = order[i]
            source, leaf = entry // per_dev, lax.rem(entry, per_dev)

            @pl.when(entry < inner_entries)
            def _():
                pltpu.make_async_copy(buffer, blocks_out.at[source, leaf], sems.at[side]).wait()

            @pl.when(entry >= inner_entries)
            def _():
                pltpu.make_async_copy(
                    buffer, other_out.at[source - 2 * per_dev, leaf], sems.at[side]
                ).wait()

        def make(i, buffer):
            entry = order[i]
            source, leaf = entry // per_dev, lax.rem(entry, per_dev)
            step = 64
            for c in range(leaf_size // step):
                at = slice(c * step, (c + 1) * step)
                hi, lo = split(matern(factors[source, at], targets[leaf]))
                buffer[0, at] = hi
                buffer[1, at] = lo

        def use(i, buffer):
            entry = order[i]
            source, leaf = entry // per_dev, lax.rem(entry, per_dev)
            field = fields[source]
            both = jnp.dot(field, buffer[0], preferred_element_type=f32)
            rest = jnp.dot(field[:vec], buffer[1], preferred_element_type=f32)
            total[leaf] += both[:vec] + both[vec:] + rest

        make(0, even)
        out_start(0, even, 0)

        def turn(i, buffer, side, last):
            @pl.when(i >= 2)
            def _():
                out_wait(i - 2, buffer, side)

            make(i, buffer)
            use(i - 1, last)
            out_start(i, buffer, side)

        def two(t, _):
            turn(2 * t + 1, odd, 1, even)

            @pl.when(2 * t + 2 < count)
            def _():
                turn(2 * t + 2, even, 0, odd)

            return 0

        lax.fori_loop(0, count // 2, two, 0)
        ends_even = lax.rem(count, 2) == 1

        @pl.when(ends_even)
        def _():
            use(count - 1, even)

        @pl.when(jnp.logical_not(ends_even))
        def _():
            use(count - 1, odd)

        group = place[1]
        mine = coarse_points[:, group]
        coarse_origin = mine[:, :1]
        target = target_factors(coordinates(mine, coarse_origin))
        for t in range(1, groups):
            far = coarse_points[:, lax.rem(group + t, groups)]
            kernel = matern(source_factors(coordinates(far, coarse_origin)), target)
            at = slice((t - 1) * coarse, t * coarse)
            couple[0, at], couple[1, at] = split(dot3_nt(kernel, transfer[0], transfer[1]))
        for leaf in range(per_dev):
            near[:, leaf_slice(leaf)] = total[leaf]
        last_even = jnp.where(ends_even, count - 1, count - 2)
        out_wait(last_even, even, 0)

        @pl.when(count >= 2)
        def _():
            out_wait(jnp.where(ends_even, count - 2, count - 1), odd, 1)

    def near_first(pair, other):
        block_shape = (2, leaf_size, leaf_size)
        return call(
            near_first_body,
            (
                field_shape,
                pltpu.HBM((2 * per_dev, *blocks_shape[1:]), bf16),
                pltpu.HBM((per_dev, *blocks_shape[1:]), bf16),
                shape(couple_shape, bf16),
            ),
            [SMEM] + [VMEM] * 5,
            (VMEM, HBM, HBM, VMEM),
            scratch=[
                pltpu.VMEM(block_shape, bf16),
                pltpu.VMEM(block_shape, bf16),
                pltpu.VMEM((3 * per_dev, leaf_size, 6 * SUB), bf16),
                pltpu.VMEM((per_dev, 6 * SUB, leaf_size), bf16),
                pltpu.VMEM((3 * per_dev, 2 * vec, leaf_size), bf16),
                pltpu.VMEM((per_dev, vec, leaf_size), f32),
                pltpu.SMEM((len(entries) + 1,), jnp.int32),
                pltpu.SemaphoreType.DMA((2,)),
            ],
            flops=10**9,
            limit=NEAR_LIMIT,
        )(near_lists, stacked, pair, other, coarse_points, transfer)

    def near_inner(field, pair, blocks):
        chosen = [entry for entry in entries if entry[0] < 2]
        shape_here = (2 * per_dev, *blocks_shape[1:])

        def body(lists, own, pair, blocks_in, near, blocks, sems):
            def in_copy(block, leaf):
                return pltpu.make_async_copy(
                    blocks_in.at[block, leaf], blocks.at[block, leaf],
                    sems.at[block * per_dev + leaf],
                )

            place = whereabouts()
            hits = [hit(place, lists, *entry) for entry in chosen]
            for (kind, j, leaf), found in zip(chosen, hits, strict=True):

                @pl.when(found)
                def _():
                    in_copy(kind * per_dev + j, leaf).start()

            near[...] = jnp.zeros_like(near)
            for (kind, j, leaf), found in zip(chosen, hits, strict=True):
                block = kind * per_dev + j

                @pl.when(found)
                def _():
                    in_copy(block, leaf).wait()
                    near[:, leaf_slice(leaf)] += dot3(
                        (own, pair)[kind][:, leaf_slice(j)],
                        blocks[block, leaf, 0],
                        blocks[block, leaf, 1],
                    )

        return call(
            body,
            field_shape,
            [SMEM, VMEM, VMEM, HBM],
            VMEM,
            scratch=[pltpu.VMEM(shape_here, bf16), pltpu.SemaphoreType.DMA((len(chosen),))],
            flops=10**8,
            limit=INNER_LIMIT,
        )(near_lists, field, pair, pltpu.with_memory_space_constraint(blocks, pltpu.HBM))

    def near_outer(other, blocks, before):
        def body(lists, other, blocks, before, near):
            near[...] = before[...]
            place = whereabouts()
            for j in range(per_dev):
                for leaf in range(per_dev):

                    @pl.when(hit(place, lists, 2, j, leaf))
                    def _():
                        near[:, leaf_slice(leaf)] += dot3(
                            other[:, leaf_slice(j)], blocks[j, leaf, 0], blocks[j, leaf, 1]
                        )

        return call(
            body,
            field_shape,
            [SMEM, VMEM, VMEM, VMEM],
            VMEM,
            flops=10**8,
            limit=limit,
        )(near_lists, other, blocks, before)

    def halo(field):
        pair = lax.ppermute(field, "leaf", inner)
        other = lax.ppermute(field, "leaf", outer)
        return pair, other

    def build_far(place, lists, received, origin, far):
        group, leaf = place[1], place[0]
        target = target_factors(coordinates(received[group * leaves + leaf, vec : vec + 3], origin))
        lane_leaf = lax.broadcasted_iota(jnp.int32, (leaves * per_dev, cols), 1) // rank
        row_leaf = lax.broadcasted_iota(jnp.int32, (leaves * per_dev, cols), 0)
        mark = jnp.zeros((leaves * per_dev, cols), f32)
        for j in range(per_dev):
            for s in range(listed):
                here = jnp.logical_and(row_leaf == lists[j, s], lane_leaf == j)
                mark = jnp.where(here, 1.0, mark)
        for i in range(leaves):
            spots = received[group * leaves + i, vec : vec + 3]
            kernel = matern(source_factors(coordinates(spots, origin)), target)
            for h in range(per_dev):
                m = i * per_dev + h
                at = slice(m * rank, (m + 1) * rank)
                hi, lo = split(kernel[h * rank : (h + 1) * rank] * mark[m : m + 1])
                far[0, at] = hi
                far[1, at] = lo

    far_shape = (2, far_rows + couple_rows, cols)

    def post_body(step, *refs):
        refs = list(refs)
        lists, couple = (refs.pop(0), refs.pop(0)) if step == 1 else (None, None)
        received, interp, near, field = refs[:4]
        refs = refs[4:]
        far, before = (None, None) if step == 1 else (refs.pop(0), refs.pop(0))
        transfer = refs.pop(0) if step < 3 else None
        out, send = refs.pop(0), refs.pop(0)
        place = whereabouts()
        group = place[1]
        if step == 1:
            far = refs.pop(0)
            origin = received[group * leaves + place[0], vec : vec + 3][:, :1]
            build_far(place, lists, received, origin, far)
            far[:, far_rows:] = couple[...]
        parts = [received[group * leaves + i, :vec] for i in range(leaves)]
        for t in range(1, groups):
            first = lax.rem(group + t, groups) * leaves
            sums = [received[first + i, :vec] for i in range(leaves)]
            while len(sums) > 1:
                sums = [sum(sums[i : i + 2]) for i in range(0, len(sums), 2)]
            parts += sums
        down = dot3(jnp.concatenate(parts, axis=1), far[0], far[1])
        news = []
        for j in range(per_dev):
            here = leaf_slice(j)
            far_part = dot3(down[:, j * rank : (j + 1) * rank], interp[0, j], interp[1, j])
            applied = (near[:, here] + far_part) * (1.0 / (leaf_size * slots))
            term = (applied - centre * field[:vec, here]) * (1.0 / half_width)
            if step > 1:
                term = 2.0 * term - before[:vec, here]
            news.append(term)
            out[:, here] = term
        if step < 3:
            own, up, sems = refs
            copies = Copies(sems)
            coeffs = coefficients(jnp.concatenate(news, axis=1), interp)
            send_all(copies, send, own, up, coeffs, transfer, group)
            copies.finish()
        else:
            squares = None
            for term in news:
                part = jnp.sum(term * term, axis=1, keepdims=True)
                squares = part if squares is None else squares + part
            diagonal = lax.broadcasted_iota(jnp.int32, (vec, 128), 0) == lax.broadcasted_iota(
                jnp.int32, (vec, 128), 1
            )
            row = jnp.sum(jnp.where(diagonal, squares, 0.0), axis=0, keepdims=True)
            for i in range(devices):
                send[i] = row

    def post(step, received, near, field, *rest):
        send_shape = (devices, vec, cols) if step < 3 else (devices, 1, 128)
        outs = [field_shape, shape(send_shape, f32)]
        specs = [VMEM, HBM if step < 3 else VMEM]
        args = [received, interp, near, field, *rest]
        if step == 1:
            outs.append(shape(far_shape, bf16))
            specs.append(VMEM)
            args = [inter_lists, couple, *args]
        scratch = []
        if step < 3:
            args.append(transfer)
            scratch = [
                pltpu.VMEM((vec, cols), f32),
                pltpu.VMEM((vec, cols), f32),
                pltpu.SemaphoreType.DMA((devices,)),
            ]
        in_specs = [VMEM] * len(args)
        if step == 1:
            in_specs[0] = SMEM
        return call(
            lambda *refs: post_body(step, *refs),
            tuple(outs),
            in_specs,
            tuple(specs),
            scratch=scratch,
            flops=10**7,
            limit=limit,
        )(*args)

    received = exchange(payload)
    pair, other = halo(stacked)
    near, blocks, other_blocks, couple = near_first(pair, other)

    def again(field):
        pair, other = halo(field)
        near = near_inner(field, pair, blocks)
        return near_outer(other, other_blocks, near)

    term_one, payload, far = post(1, received, near, stacked)
    received = exchange(payload)
    near = again(term_one)
    term_two, payload = post(2, received, near, term_one, far, stacked)
    received = exchange(payload)
    near = again(term_two)
    term_three, payload = post(3, received, near, term_two, far, term_one)
    received = exchange(payload)
    squares = jnp.sum(received, axis=(0, 1))[:vec]
    total_points = width * devices
    return term_three / jnp.sqrt(squares / total_points + 1e-06)[:, None]


def solution(mesh):
    placed = (
        P(None, ("grp", "leaf")),
        P(None, ("grp", "leaf")),
        P(("grp", "leaf"), None),
        P(("grp", "leaf"), None),
        P(("grp", "leaf"), None),
        P(("grp", "leaf"), None, None),
        P(("grp", "leaf"), None, None),
        P(),
    )

    return jax.shard_map(
        on_device, mesh=mesh, in_specs=placed, out_specs=P(None, ("grp", "leaf")), check_vma=False
    )
```

```python
import jax
import jax.numpy as jnp
from jax import lax
from jax.experimental import pallas as pl
from jax.experimental.pallas import tpu as pltpu
from jax.sharding import PartitionSpec as P

kappa_scale = 3.4641016151377544
log2_e = 1.4426950408889634
centre = 0.05
half_width = 0.05
f32 = jnp.float32
bf16 = jnp.bfloat16

HBM = pl.BlockSpec(memory_space=pltpu.HBM)
VMEM = pl.BlockSpec(memory_space=pltpu.VMEM)
SMEM = pl.BlockSpec(memory_space=pltpu.SMEM)
SUB = 8
NEAR_LIMIT = 54000
INNER_LIMIT = 16000
START_LIMIT = 6000


def split(x):
    hi = x.astype(bf16)
    return hi, (x - hi.astype(f32)).astype(bf16)


def dot3(left, right_hi, right_lo):
    rows = left.shape[0]
    hi, lo = split(left)
    both = jnp.dot(jnp.concatenate([hi, lo], axis=0), right_hi, preferred_element_type=f32)
    return both[:rows] + both[rows:] + jnp.dot(hi, right_lo, preferred_element_type=f32)


def dot3_nt(left, right_hi, right_lo):
    rows = left.shape[0]
    hi, lo = split(left)
    dot = lambda a, b: lax.dot_general(
        a, b, (((1,), (1,)), ((), ())), preferred_element_type=f32
    )
    both = dot(jnp.concatenate([hi, lo], axis=0), right_hi)
    return both[:rows] + both[rows:] + dot(hi, right_lo)


def three_parts(x):
    first = x.astype(bf16).astype(f32)
    second = (x - first).astype(bf16).astype(f32)
    return first, second, x - first - second


def distance_factors(points):
    x, y, z = points
    n = x.shape[1]
    norm = x * x + y * y + z * z
    at = lax.broadcasted_iota(jnp.int32, (SUB, n), 0)

    def rows(values):
        out = jnp.zeros((SUB, n), f32)
        for i, value in enumerate(values):
            out = jnp.where(at == i, value, out)
        return three_parts(out)

    s1, s2, s3 = rows([x, y, z, norm, 1.0])
    t1, t2, t3 = rows([-2.0 * x, -2.0 * y, -2.0 * z, 1.0, norm])
    source = jnp.concatenate([s1, s1, s2, s1, s3, s2], axis=0)
    target = jnp.concatenate([t1, t2, t1, t3, t1, t2], axis=0)
    return source, target


def source_factors(points):
    return distance_factors(points)[0].astype(bf16).T


def target_factors(points):
    return distance_factors(points)[1].astype(bf16)


def matern(source, target):
    square = jnp.maximum(jnp.dot(source, target, preferred_element_type=f32), 1e-30)
    scaled = square * lax.rsqrt(square)
    return (1.0 + scaled) * jnp.exp2(scaled * -log2_e)


def coordinates(points, origin):
    return [(points[d : d + 1] - origin[d : d + 1, :1]) * kappa_scale for d in range(3)]


class Copies:
    def __init__(self, sems):
        self.sems, self.used, self.open = sems, 0, {}

    def start(self, name, source, target):
        copy = pltpu.make_async_copy(source, target, self.sems.at[self.used])
        self.used += 1
        copy.start()
        self.open[name] = copy

    def wait(self, *names):
        for name in names:
            self.open.pop(name).wait()

    def finish(self):
        self.wait(*list(self.open))


def call(kernel, out_shape, in_specs, out_specs, scratch=(), flops=0, limit=60 * 1024):
    return pl.pallas_call(
        kernel,
        out_shape=out_shape,
        in_specs=in_specs,
        out_specs=out_specs,
        scratch_shapes=scratch,
        compiler_params=pltpu.CompilerParams(vmem_limit_bytes=limit << 10),
        cost_estimate=pl.CostEstimate(flops=flops, bytes_accessed=1 << 20, transcendentals=0),
    )


def on_device(vectors, points, near_lists, inter_lists, skeleton, interp, transfer, coarse_points):
    per_dev, slots = near_lists.shape
    listed = inter_lists.shape[1]
    rank, leaf_size = interp.shape[1:]
    coarse = transfer.shape[2]
    vec, width = vectors.shape
    leaves, groups = lax.axis_size("leaf"), lax.axis_size("grp")
    devices = leaves * groups
    cols = per_dev * rank
    assert cols == coarse
    transfer = transfer.reshape(cols, coarse)
    inner = [(i, i ^ 1) for i in range(leaves)]
    outer = [(i, i + 1) for i in range(1, leaves - 1, 2)]
    outer = outer + [(j, i) for i, j in outer]
    exchange = lambda x: lax.all_to_all(x, ("grp", "leaf"), 0, 0, tiled=True)
    shape = jax.ShapeDtypeStruct
    field_shape = shape((vec, width), f32)
    couple_rows = (groups - 1) * coarse
    far_rows = leaves * cols
    limit = max(6000, far_rows * 3 // 2)
    leaf_slice = lambda j: slice(j * leaf_size, (j + 1) * leaf_size)

    def whereabouts():
        return lax.axis_index("leaf"), lax.axis_index("grp")

    def hit(place, lists, kind, j, leaf):
        odd = lax.rem(place[0], 2)
        if kind == 0:
            spot = per_dev + j
        else:
            spot = jnp.where(odd == kind - 1, 2 * per_dev, 0) + j
        found = lists[leaf, 0] == spot
        for slot in range(1, slots):
            found = jnp.logical_or(found, lists[leaf, slot] == spot)
        return found

    def coefficients(field, interp):
        return jnp.concatenate(
            [
                dot3_nt(field[:, leaf_slice(j)], interp[0, j], interp[1, j])
                for j in range(per_dev)
            ],
            axis=1,
        )

    def send_all(copies, out, own, up, coeffs, transfer, group):
        own[:vec] = coeffs
        for i in range(leaves):
            copies.start(("own", i), own, out.at[group * leaves + i])
        up[:vec] = dot3(coeffs, transfer[0], transfer[1])
        for t in range(1, groups):
            first = lax.rem(group + t, groups) * leaves
            for i in range(leaves):
                copies.start(("up", t, i), up, out.at[first + i])

    def start_body(
        field_in, points_in, skel_in, interp_in, transfer_in, coarse_in, near_lists_in, inter_lists_in,
        out, stacked, interp, transfer, coarse_points, near_lists, inter_lists,
        points, skel, whole_interp, whole_transfer, own, up, sems,
    ):
        field = stacked.at[pl.ds(0, vec)]
        copies = Copies(sems)
        copies.start("points", points_in, points)
        copies.start("skel", skel_in, skel)
        copies.start("field", field_in, field)
        copies.start("interp", interp_in, whole_interp)
        copies.start("transfer", transfer_in, whole_transfer)
        copies.start("coarse", coarse_in, coarse_points)
        copies.start("near_lists", near_lists_in, near_lists)
        copies.start("inter_lists", inter_lists_in, inter_lists)
        own[vec:] = jnp.zeros((SUB, cols), f32)
        up[vec:] = jnp.zeros((SUB, cols), f32)
        copies.wait("points", "skel")
        stacked[vec:] = jnp.zeros((SUB, width), f32)
        stacked[vec : vec + 3] = points[...]
        for j in range(per_dev):
            places = lax.broadcasted_iota(jnp.int32, (leaf_size, rank), 0)
            pick = (places == skel[j : j + 1, :]).astype(f32).astype(bf16)
            parts = jnp.concatenate(
                three_parts(stacked[vec:, leaf_slice(j)]), axis=0
            ).astype(bf16)
            spots = jnp.dot(parts, pick, preferred_element_type=f32)
            spots = spots[:SUB] + spots[SUB : 2 * SUB] + spots[2 * SUB :]
            own[vec:, j * rank : (j + 1) * rank] = spots
        copies.wait("interp", "field")
        for j in range(per_dev):
            interp[0, j], interp[1, j] = split(whole_interp[j])
        coeffs = coefficients(field, interp)
        copies.wait("transfer")
        transfer[0], transfer[1] = split(whole_transfer[...])
        send_all(copies, out, own, up, coeffs, transfer, whereabouts()[1])
        copies.finish()

    payload, stacked, interp, transfer, coarse_points, near_lists, inter_lists = call(
        start_body,
        (
            shape((devices, vec + SUB, cols), f32),
            shape((vec + SUB, width), f32),
            shape((2, *interp.shape), bf16),
            shape((2, *transfer.shape), bf16),
            shape((3, groups, coarse), f32),
            shape(near_lists.shape, jnp.int32),
            shape(inter_lists.shape, jnp.int32),
        ),
        [HBM] * 8,
        (HBM,) + (VMEM,) * 6,
        scratch=[
            pltpu.VMEM((3, width), f32),
            pltpu.VMEM((per_dev, rank), jnp.int32),
            pltpu.VMEM(interp.shape, f32),
            pltpu.VMEM(transfer.shape, f32),
            pltpu.VMEM((vec + SUB, cols), f32),
            pltpu.VMEM((vec + SUB, cols), f32),
            pltpu.SemaphoreType.DMA((8 + devices,)),
        ],
        flops=10**7,
        limit=START_LIMIT,
    )(
        *[
            pltpu.with_memory_space_constraint(x, pltpu.HBM)
            for x in (
                vectors, points, skeleton, interp, transfer, coarse_points.transpose(1, 0, 2),
                near_lists, inter_lists,
            )
        ]
    )
    entries = [
        (kind, j, leaf) for kind in range(3) for j in range(per_dev) for leaf in range(per_dev)
    ]
    blocks_shape = (3 * per_dev, per_dev, 2, leaf_size, leaf_size)
    couple_shape = (2, couple_rows, cols)

    def near_first_body(
        lists, inter_lists, own, pair, other, coarse_points, transfer,
        near, blocks_out, other_out, couple, marks,
        even, odd, factors, targets, fields, total, order, sems,
    ):
        place = whereabouts()
        origin = own[vec : vec + 3][:, :1]
        for leaf in range(per_dev):
            targets[leaf] = target_factors(coordinates(own[vec : vec + 3, leaf_slice(leaf)], origin))
            total[leaf] = jnp.zeros((vec, leaf_size), f32)
        count = jnp.int32(0)
        for i, (kind, j, leaf) in enumerate(entries):
            window = (own, pair, other)[kind]
            if leaf == 0:
                source = kind * per_dev + j
                factors[source] = source_factors(
                    coordinates(window[vec : vec + 3, leaf_slice(j)], origin)
                )
                fields[source] = jnp.concatenate(split(window[:vec, leaf_slice(j)]), axis=0)
            order[count] = i
            count = count + hit(place, lists, kind, j, leaf).astype(jnp.int32)

        inner_entries = 2 * per_dev * per_dev

        def out_start(i, buffer, side):
            entry = order[i]
            source, leaf = entry // per_dev, lax.rem(entry, per_dev)

            @pl.when(entry < inner_entries)
            def _():
                pltpu.make_async_copy(buffer, blocks_out.at[source, leaf], sems.at[side]).start()

            @pl.when(entry >= inner_entries)
            def _():
                pltpu.make_async_copy(
                    buffer, other_out.at[source - 2 * per_dev, leaf], sems.at[side]
                ).start()

        def out_wait(i, buffer, side):
            entry = order[i]
            source, leaf = entry // per_dev, lax.rem(entry, per_dev)

            @pl.when(entry < inner_entries)
            def _():
                pltpu.make_async_copy(buffer, blocks_out.at[source, leaf], sems.at[side]).wait()

            @pl.when(entry >= inner_entries)
            def _():
                pltpu.make_async_copy(
                    buffer, other_out.at[source - 2 * per_dev, leaf], sems.at[side]
                ).wait()

        def make(i, buffer):
            entry = order[i]
            source, leaf = entry // per_dev, lax.rem(entry, per_dev)
            step = 64
            for c in range(leaf_size // step):
                at = slice(c * step, (c + 1) * step)
                hi, lo = split(matern(factors[source, at], targets[leaf]))
                buffer[0, at] = hi
                buffer[1, at] = lo

        def use(i, buffer):
            entry = order[i]
            source, leaf = entry // per_dev, lax.rem(entry, per_dev)
            field = fields[source]
            both = jnp.dot(field, buffer[0], preferred_element_type=f32)
            rest = jnp.dot(field[:vec], buffer[1], preferred_element_type=f32)
            total[leaf] += both[:vec] + both[vec:] + rest

        make(0, even)
        out_start(0, even, 0)

        def turn(i, buffer, side, last):
            @pl.when(i >= 2)
            def _():
                out_wait(i - 2, buffer, side)

            make(i, buffer)
            use(i - 1, last)
            out_start(i, buffer, side)

        def two(t, _):
            turn(2 * t + 1, odd, 1, even)

            @pl.when(2 * t + 2 < count)
            def _():
                turn(2 * t + 2, even, 0, odd)

            return 0

        lax.fori_loop(0, count // 2, two, 0)
        ends_even = lax.rem(count, 2) == 1

        @pl.when(ends_even)
        def _():
            use(count - 1, even)

        @pl.when(jnp.logical_not(ends_even))
        def _():
            use(count - 1, odd)

        group = place[1]
        mine = coarse_points[:, group]
        coarse_origin = mine[:, :1]
        target = target_factors(coordinates(mine, coarse_origin))
        for t in range(1, groups):
            far = coarse_points[:, lax.rem(group + t, groups)]
            kernel = matern(source_factors(coordinates(far, coarse_origin)), target)
            at = slice((t - 1) * coarse, t * coarse)
            couple[0, at], couple[1, at] = split(dot3_nt(kernel, transfer[0], transfer[1]))
        lane_leaf = lax.broadcasted_iota(jnp.int32, marks.shape, 1) // rank
        row_leaf = lax.broadcasted_iota(jnp.int32, marks.shape, 0)
        mark = jnp.zeros(marks.shape, f32)
        for j in range(per_dev):
            for s in range(listed):
                chosen = jnp.logical_and(row_leaf == inter_lists[j, s], lane_leaf == j)
                mark = jnp.where(chosen, 1.0, mark)
        marks[...] = mark
        for leaf in range(per_dev):
            near[:, leaf_slice(leaf)] = total[leaf]
        last_even = jnp.where(ends_even, count - 1, count - 2)
        out_wait(last_even, even, 0)

        @pl.when(count >= 2)
        def _():
            out_wait(jnp.where(ends_even, count - 2, count - 1), odd, 1)

    def near_first(pair, other):
        block_shape = (2, leaf_size, leaf_size)
        return call(
            near_first_body,
            (
                field_shape,
                pltpu.HBM((2 * per_dev, *blocks_shape[1:]), bf16),
                pltpu.HBM((per_dev, *blocks_shape[1:]), bf16),
                shape(couple_shape, bf16),
                shape((leaves * per_dev, cols), f32),
            ),
            [SMEM, SMEM] + [VMEM] * 5,
            (VMEM, HBM, HBM, VMEM, VMEM),
            scratch=[
                pltpu.VMEM(block_shape, bf16),
                pltpu.VMEM(block_shape, bf16),
                pltpu.VMEM((3 * per_dev, leaf_size, 6 * SUB), bf16),
                pltpu.VMEM((per_dev, 6 * SUB, leaf_size), bf16),
                pltpu.VMEM((3 * per_dev, 2 * vec, leaf_size), bf16),
                pltpu.VMEM((per_dev, vec, leaf_size), f32),
                pltpu.SMEM((len(entries) + 1,), jnp.int32),
                pltpu.SemaphoreType.DMA((2,)),
            ],
            flops=10**9,
            limit=NEAR_LIMIT,
        )(near_lists, inter_lists, stacked, pair, other, coarse_points, transfer)

    def near_inner(field, pair, blocks):
        chosen = [entry for entry in entries if entry[0] < 2]
        shape_here = (2 * per_dev, *blocks_shape[1:])

        def body(lists, own, pair, blocks_in, near, blocks, sems):
            def in_copy(block, leaf):
                return pltpu.make_async_copy(
                    blocks_in.at[block, leaf], blocks.at[block, leaf],
                    sems.at[block * per_dev + leaf],
                )

            place = whereabouts()
            hits = [hit(place, lists, *entry) for entry in chosen]
            for (kind, j, leaf), found in zip(chosen, hits, strict=True):

                @pl.when(found)
                def _():
                    in_copy(kind * per_dev + j, leaf).start()

            near[...] = jnp.zeros_like(near)
            for (kind, j, leaf), found in zip(chosen, hits, strict=True):
                block = kind * per_dev + j

                @pl.when(found)
                def _():
                    in_copy(block, leaf).wait()
                    near[:, leaf_slice(leaf)] += dot3(
                        (own, pair)[kind][:, leaf_slice(j)],
                        blocks[block, leaf, 0],
                        blocks[block, leaf, 1],
                    )

        return call(
            body,
            field_shape,
            [SMEM, VMEM, VMEM, HBM],
            VMEM,
            scratch=[pltpu.VMEM(shape_here, bf16), pltpu.SemaphoreType.DMA((len(chosen),))],
            flops=10**8,
            limit=INNER_LIMIT,
        )(near_lists, field, pair, pltpu.with_memory_space_constraint(blocks, pltpu.HBM))

    def near_outer(other, blocks, before):
        def body(lists, other, blocks, before, near):
            near[...] = before[...]
            place = whereabouts()
            for j in range(per_dev):
                for leaf in range(per_dev):

                    @pl.when(hit(place, lists, 2, j, leaf))
                    def _():
                        near[:, leaf_slice(leaf)] += dot3(
                            other[:, leaf_slice(j)], blocks[j, leaf, 0], blocks[j, leaf, 1]
                        )

        return call(
            body,
            field_shape,
            [SMEM, VMEM, VMEM, VMEM],
            VMEM,
            flops=10**8,
            limit=limit,
        )(near_lists, other, blocks, before)

    def halo(field):
        pair = lax.ppermute(field, "leaf", inner)
        other = lax.ppermute(field, "leaf", outer)
        return pair, other

    def build_far(place, marks, received, origin, far):
        group, leaf = place[1], place[0]
        target = target_factors(coordinates(received[group * leaves + leaf, vec : vec + 3], origin))
        for i in range(leaves):
            spots = received[group * leaves + i, vec : vec + 3]
            kernel = matern(source_factors(coordinates(spots, origin)), target)
            for h in range(per_dev):
                m = i * per_dev + h
                at = slice(m * rank, (m + 1) * rank)
                hi, lo = split(kernel[h * rank : (h + 1) * rank] * marks[m : m + 1])
                far[0, at] = hi
                far[1, at] = lo

    far_shape = (2, far_rows + couple_rows, cols)

    def post_body(step, *refs):
        refs = list(refs)
        marks, couple = (refs.pop(0), refs.pop(0)) if step == 1 else (None, None)
        received, interp, near, field = refs[:4]
        refs = refs[4:]
        far, before = (None, None) if step == 1 else (refs.pop(0), refs.pop(0))
        transfer = refs.pop(0) if step < 3 else None
        out, send = refs.pop(0), refs.pop(0)
        place = whereabouts()
        group = place[1]
        if step == 1:
            far = refs.pop(0)
            origin = received[group * leaves + place[0], vec : vec + 3][:, :1]
            build_far(place, marks, received, origin, far)
            far[:, far_rows:] = couple[...]
        parts = [received[group * leaves + i, :vec] for i in range(leaves)]
        for t in range(1, groups):
            first = lax.rem(group + t, groups) * leaves
            sums = [received[first + i, :vec] for i in range(leaves)]
            while len(sums) > 1:
                sums = [sum(sums[i : i + 2]) for i in range(0, len(sums), 2)]
            parts += sums
        down = dot3(jnp.concatenate(parts, axis=1), far[0], far[1])
        news = []
        for j in range(per_dev):
            here = leaf_slice(j)
            far_part = dot3(down[:, j * rank : (j + 1) * rank], interp[0, j], interp[1, j])
            applied = (near[:, here] + far_part) * (1.0 / (leaf_size * slots))
            term = (applied - centre * field[:vec, here]) * (1.0 / half_width)
            if step > 1:
                term = 2.0 * term - before[:vec, here]
            news.append(term)
            out[:, here] = term
        if step < 3:
            own, up, sems = refs
            copies = Copies(sems)
            coeffs = coefficients(jnp.concatenate(news, axis=1), interp)
            send_all(copies, send, own, up, coeffs, transfer, group)
            copies.finish()
        else:
            squares = None
            for term in news:
                part = jnp.sum(term * term, axis=1, keepdims=True)
                squares = part if squares is None else squares + part
            diagonal = lax.broadcasted_iota(jnp.int32, (vec, 128), 0) == lax.broadcasted_iota(
                jnp.int32, (vec, 128), 1
            )
            row = jnp.sum(jnp.where(diagonal, squares, 0.0), axis=0, keepdims=True)
            for i in range(devices):
                send[i] = row

    def post(step, received, near, field, *rest):
        send_shape = (devices, vec, cols) if step < 3 else (devices, 1, 128)
        outs = [field_shape, shape(send_shape, f32)]
        specs = [VMEM, HBM if step < 3 else VMEM]
        args = [received, interp, near, field, *rest]
        if step == 1:
            outs.append(shape(far_shape, bf16))
            specs.append(VMEM)
            args = [marks, couple, *args]
        scratch = []
        if step < 3:
            args.append(transfer)
            scratch = [
                pltpu.VMEM((vec, cols), f32),
                pltpu.VMEM((vec, cols), f32),
                pltpu.SemaphoreType.DMA((devices,)),
            ]
        return call(
            lambda *refs: post_body(step, *refs),
            tuple(outs),
            [VMEM] * len(args),
            tuple(specs),
            scratch=scratch,
            flops=10**7,
            limit=limit,
        )(*args)

    received = exchange(payload)
    pair, other = halo(stacked)
    near, blocks, other_blocks, couple, marks = near_first(pair, other)

    def again(field):
        pair, other = halo(field)
        near = near_inner(field, pair, blocks)
        return near_outer(other, other_blocks, near)

    term_one, payload, far = post(1, received, near, stacked)
    received = exchange(payload)
    near = again(term_one)
    term_two, payload = post(2, received, near, term_one, far, stacked)
    received = exchange(payload)
    near = again(term_two)
    term_three, payload = post(3, received, near, term_two, far, term_one)
    received = exchange(payload)
    squares = jnp.sum(received, axis=(0, 1))[:vec]
    total_points = width * devices
    return term_three / jnp.sqrt(squares / total_points + 1e-06)[:, None]


def solution(mesh):
    placed = (
        P(None, ("grp", "leaf")),
        P(None, ("grp", "leaf")),
        P(("grp", "leaf"), None),
        P(("grp", "leaf"), None),
        P(("grp", "leaf"), None),
        P(("grp", "leaf"), None, None),
        P(("grp", "leaf"), None, None),
        P(),
    )

    return jax.shard_map(
        on_device, mesh=mesh, in_specs=placed, out_specs=P(None, ("grp", "leaf")), check_vma=False
    )
```

```python
import jax
import jax.numpy as jnp
from jax import lax
from jax.experimental import pallas as pl
from jax.experimental.pallas import tpu as pltpu
from jax.sharding import PartitionSpec as P

kappa_scale = 3.4641016151377544
log2_e = 1.4426950408889634
centre = 0.05
half_width = 0.05
f32 = jnp.float32
bf16 = jnp.bfloat16

HBM = pl.BlockSpec(memory_space=pltpu.HBM)
VMEM = pl.BlockSpec(memory_space=pltpu.VMEM)
SMEM = pl.BlockSpec(memory_space=pltpu.SMEM)
SUB = 8
NEAR_LIMIT = 54000
INNER_LIMIT = 16000
START_LIMIT = 6000


def split(x):
    hi = x.astype(bf16)
    return hi, (x - hi.astype(f32)).astype(bf16)


def dot3(left, right_hi, right_lo):
    rows = left.shape[0]
    hi, lo = split(left)
    both = jnp.dot(jnp.concatenate([hi, lo], axis=0), right_hi, preferred_element_type=f32)
    return both[:rows] + both[rows:] + jnp.dot(hi, right_lo, preferred_element_type=f32)


def dot3_nt(left, right_hi, right_lo):
    rows = left.shape[0]
    hi, lo = split(left)
    dot = lambda a, b: lax.dot_general(
        a, b, (((1,), (1,)), ((), ())), preferred_element_type=f32
    )
    both = dot(jnp.concatenate([hi, lo], axis=0), right_hi)
    return both[:rows] + both[rows:] + dot(hi, right_lo)


def three_parts(x):
    first = x.astype(bf16).astype(f32)
    second = (x - first).astype(bf16).astype(f32)
    return first, second, x - first - second


def distance_factors(points):
    x, y, z = points
    n = x.shape[1]
    norm = x * x + y * y + z * z
    at = lax.broadcasted_iota(jnp.int32, (SUB, n), 0)

    def rows(values):
        out = jnp.zeros((SUB, n), f32)
        for i, value in enumerate(values):
            out = jnp.where(at == i, value, out)
        return three_parts(out)

    s1, s2, s3 = rows([x, y, z, norm, 1.0])
    t1, t2, t3 = rows([-2.0 * x, -2.0 * y, -2.0 * z, 1.0, norm])
    source = jnp.concatenate([s1, s1, s2, s1, s3, s2], axis=0)
    target = jnp.concatenate([t1, t2, t1, t3, t1, t2], axis=0)
    return source, target


def source_factors(points):
    return distance_factors(points)[0].astype(bf16).T


def target_factors(points):
    return distance_factors(points)[1].astype(bf16)


def matern(source, target):
    square = jnp.maximum(jnp.dot(source, target, preferred_element_type=f32), 1e-30)
    scaled = square * lax.rsqrt(square)
    return (1.0 + scaled) * jnp.exp2(scaled * -log2_e)


def coordinates(points, origin):
    return [(points[d : d + 1] - origin[d : d + 1, :1]) * kappa_scale for d in range(3)]


class Copies:
    def __init__(self, sems):
        self.sems, self.used, self.open = sems, 0, {}

    def start(self, name, source, target):
        copy = pltpu.make_async_copy(source, target, self.sems.at[self.used])
        self.used += 1
        copy.start()
        self.open[name] = copy

    def wait(self, *names):
        for name in names:
            self.open.pop(name).wait()

    def finish(self):
        self.wait(*list(self.open))


def call(kernel, out_shape, in_specs, out_specs, scratch=(), flops=0, limit=60 * 1024):
    return pl.pallas_call(
        kernel,
        out_shape=out_shape,
        in_specs=in_specs,
        out_specs=out_specs,
        scratch_shapes=scratch,
        compiler_params=pltpu.CompilerParams(vmem_limit_bytes=limit << 10),
        cost_estimate=pl.CostEstimate(flops=flops, bytes_accessed=1 << 20, transcendentals=0),
    )


def on_device(vectors, points, near_lists, inter_lists, skeleton, interp, transfer, coarse_points):
    per_dev, slots = near_lists.shape
    listed = inter_lists.shape[1]
    rank, leaf_size = interp.shape[1:]
    coarse = transfer.shape[2]
    vec, width = vectors.shape
    leaves, groups = lax.axis_size("leaf"), lax.axis_size("grp")
    devices = leaves * groups
    cols = per_dev * rank
    assert cols == coarse
    transfer = transfer.reshape(cols, coarse)
    inner = [(i, i ^ 1) for i in range(leaves)]
    outer = [(i, i + 1) for i in range(1, leaves - 1, 2)]
    outer = outer + [(j, i) for i, j in outer]
    exchange = lambda x: lax.all_to_all(x, ("grp", "leaf"), 0, 0, tiled=True)
    shape = jax.ShapeDtypeStruct
    field_shape = shape((vec, width), f32)
    couple_rows = (groups - 1) * coarse
    far_rows = leaves * cols
    pieces = vec // 2
    wide = (pieces + 2) * cols
    piece = lambda k: slice(k * cols, (k + 1) * cols)
    limit = max(6000, far_rows * 3 // 2)
    leaf_slice = lambda j: slice(j * leaf_size, (j + 1) * leaf_size)

    def whereabouts():
        return lax.axis_index("leaf"), lax.axis_index("grp")

    def hit(place, lists, kind, j, leaf):
        odd = lax.rem(place[0], 2)
        if kind == 0:
            spot = per_dev + j
        else:
            spot = jnp.where(odd == kind - 1, 2 * per_dev, 0) + j
        found = lists[leaf, 0] == spot
        for slot in range(1, slots):
            found = jnp.logical_or(found, lists[leaf, slot] == spot)
        return found

    def coefficients(field, interp):
        return jnp.concatenate(
            [
                dot3_nt(field[:, leaf_slice(j)], interp[0, j], interp[1, j])
                for j in range(per_dev)
            ],
            axis=1,
        )

    def put_rows(block, values):
        if block.shape[0] == vec:
            block[...] = values
        else:
            for k in range(pieces):
                block[:, piece(k)] = values[2 * k : 2 * k + 2]

    def send_all(copies, out, own, up, coeffs, transfer, group):
        put_rows(own, coeffs)
        for i in range(leaves):
            copies.start(("own", i), own, out.at[group * leaves + i])
        put_rows(up, dot3(coeffs, transfer[0], transfer[1]))
        for t in range(1, groups):
            first = lax.rem(group + t, groups) * leaves
            for i in range(leaves):
                copies.start(("up", t, i), up, out.at[first + i])

    def start_body(
        field_in, points_in, skel_in, interp_in, transfer_in, coarse_in, near_lists_in, inter_lists_in,
        out, stacked, interp, transfer, coarse_points, near_lists, inter_lists,
        points, skel, whole_interp, whole_transfer, own, up, sems,
    ):
        field = stacked.at[pl.ds(0, vec)]
        copies = Copies(sems)
        copies.start("points", points_in, points)
        copies.start("skel", skel_in, skel)
        copies.start("field", field_in, field)
        copies.start("interp", interp_in, whole_interp)
        copies.start("transfer", transfer_in, whole_transfer)
        copies.start("coarse", coarse_in, coarse_points)
        copies.start("near_lists", near_lists_in, near_lists)
        copies.start("inter_lists", inter_lists_in, inter_lists)
        up[:, piece(pieces)] = jnp.zeros((2, cols), f32)
        up[:, piece(pieces + 1)] = jnp.zeros((2, cols), f32)
        copies.wait("points", "skel")
        stacked[vec:] = jnp.zeros((SUB, width), f32)
        stacked[vec : vec + 3] = points[...]
        all_spots = []
        for j in range(per_dev):
            places = lax.broadcasted_iota(jnp.int32, (leaf_size, rank), 0)
            pick = (places == skel[j : j + 1, :]).astype(f32).astype(bf16)
            parts = jnp.concatenate(
                three_parts(stacked[vec:, leaf_slice(j)]), axis=0
            ).astype(bf16)
            spots = jnp.dot(parts, pick, preferred_element_type=f32)
            spots = spots[:SUB] + spots[SUB : 2 * SUB] + spots[2 * SUB :]
            all_spots.append(spots)
        all_spots = jnp.concatenate(all_spots, axis=1)
        own[:, piece(pieces)] = all_spots[:2]
        own[:, piece(pieces + 1)] = all_spots[2:4]
        copies.wait("interp", "field")
        for j in range(per_dev):
            interp[0, j], interp[1, j] = split(whole_interp[j])
        coeffs = coefficients(field, interp)
        copies.wait("transfer")
        transfer[0], transfer[1] = split(whole_transfer[...])
        send_all(copies, out, own, up, coeffs, transfer, whereabouts()[1])
        copies.finish()

    payload, stacked, interp, transfer, coarse_points, near_lists, inter_lists = call(
        start_body,
        (
            shape((devices, 2, wide), f32),
            shape((vec + SUB, width), f32),
            shape((2, *interp.shape), bf16),
            shape((2, *transfer.shape), bf16),
            shape((3, groups, coarse), f32),
            shape(near_lists.shape, jnp.int32),
            shape(inter_lists.shape, jnp.int32),
        ),
        [HBM] * 8,
        (HBM,) + (VMEM,) * 6,
        scratch=[
            pltpu.VMEM((3, width), f32),
            pltpu.VMEM((per_dev, rank), jnp.int32),
            pltpu.VMEM(interp.shape, f32),
            pltpu.VMEM(transfer.shape, f32),
            pltpu.VMEM((2, wide), f32),
            pltpu.VMEM((2, wide), f32),
            pltpu.SemaphoreType.DMA((8 + devices,)),
        ],
        flops=10**7,
        limit=START_LIMIT,
    )(
        *[
            pltpu.with_memory_space_constraint(x, pltpu.HBM)
            for x in (
                vectors, points, skeleton, interp, transfer, coarse_points.transpose(1, 0, 2),
                near_lists, inter_lists,
            )
        ]
    )
    entries = [
        (kind, j, leaf) for kind in range(3) for j in range(per_dev) for leaf in range(per_dev)
    ]
    blocks_shape = (3 * per_dev, per_dev, 2, leaf_size, leaf_size)
    couple_shape = (2, couple_rows, cols)

    mirrored, mirror = (0, 1, 0), (0, 0, 1)

    def both_ways(place, lists):
        return jnp.logical_and(hit(place, lists, *mirrored), hit(place, lists, *mirror))

    def near_first_body(
        lists, inter_lists, own, pair, other, coarse_points, transfer,
        near, blocks_out, other_out, couple, marks,
        even, odd, factors, targets, fields, total, order, sems,
    ):
        place = whereabouts()
        origin = own[vec : vec + 3][:, :1]
        for leaf in range(per_dev):
            targets[leaf] = target_factors(coordinates(own[vec : vec + 3, leaf_slice(leaf)], origin))
            total[leaf] = jnp.zeros((vec, leaf_size), f32)
        for kind, window in enumerate((own, pair, other)):
            for j in range(per_dev):
                source = kind * per_dev + j
                factors[source] = source_factors(
                    coordinates(window[vec : vec + 3, leaf_slice(j)], origin)
                )
                fields[source] = jnp.concatenate(split(window[:vec, leaf_slice(j)]), axis=0)
        twice = both_ways(place, lists)
        count = jnp.int32(0)
        for entry in [mirror] + [entry for entry in entries if entry != mirror]:
            found = hit(place, lists, *entry)
            if entry == mirrored:
                found = jnp.logical_and(found, jnp.logical_not(twice))
            order[count] = entries.index(entry)
            count = count + found.astype(jnp.int32)

        inner_entries = 2 * per_dev * per_dev

        def out_start(i, buffer, side):
            entry = order[i]
            source, leaf = entry // per_dev, lax.rem(entry, per_dev)

            @pl.when(entry < inner_entries)
            def _():
                pltpu.make_async_copy(buffer, blocks_out.at[source, leaf], sems.at[side]).start()

            @pl.when(entry >= inner_entries)
            def _():
                pltpu.make_async_copy(
                    buffer, other_out.at[source - 2 * per_dev, leaf], sems.at[side]
                ).start()

        def out_wait(i, buffer, side):
            entry = order[i]
            source, leaf = entry // per_dev, lax.rem(entry, per_dev)

            @pl.when(entry < inner_entries)
            def _():
                pltpu.make_async_copy(buffer, blocks_out.at[source, leaf], sems.at[side]).wait()

            @pl.when(entry >= inner_entries)
            def _():
                pltpu.make_async_copy(
                    buffer, other_out.at[source - 2 * per_dev, leaf], sems.at[side]
                ).wait()

        def make(i, buffer):
            entry = order[i]
            source, leaf = entry // per_dev, lax.rem(entry, per_dev)
            step = 64
            for c in range(leaf_size // step):
                at = slice(c * step, (c + 1) * step)
                hi, lo = split(matern(factors[source, at], targets[leaf]))
                buffer[0, at] = hi
                buffer[1, at] = lo

        def use(i, buffer):
            entry = order[i]
            source, leaf = entry // per_dev, lax.rem(entry, per_dev)
            field = fields[source]
            both = jnp.dot(field, buffer[0], preferred_element_type=f32)
            rest = jnp.dot(field[:vec], buffer[1], preferred_element_type=f32)
            total[leaf] += both[:vec] + both[vec:] + rest

        group = place[1]
        mine = coarse_points[:, group]
        coarse_origin = mine[:, :1]
        target = target_factors(coordinates(mine, coarse_origin))
        for t in range(1, groups):
            far = coarse_points[:, lax.rem(group + t, groups)]
            kernel = matern(source_factors(coordinates(far, coarse_origin)), target)
            at = slice((t - 1) * coarse, t * coarse)
            couple[0, at], couple[1, at] = split(dot3_nt(kernel, transfer[0], transfer[1]))
        lane_leaf = lax.broadcasted_iota(jnp.int32, marks.shape, 1) // rank
        row_leaf = lax.broadcasted_iota(jnp.int32, marks.shape, 0)
        mark = jnp.zeros(marks.shape, f32)
        for j in range(per_dev):
            for s in range(listed):
                chosen = jnp.logical_and(row_leaf == inter_lists[j, s], lane_leaf == j)
                mark = jnp.where(chosen, 1.0, mark)
        marks[...] = mark
        make(0, even)
        out_start(0, even, 0)

        @pl.when(twice)
        def _():
            across = lambda a, b: lax.dot_general(
                a, b, (((1,), (1,)), ((), ())), preferred_element_type=f32
            )
            both = across(fields[1], even[0])
            total[0] += both[:vec] + both[vec:] + across(fields[1, :vec], even[1])


        def turn(i, buffer, side, last):
            @pl.when(i >= 2)
            def _():
                out_wait(i - 2, buffer, side)

            make(i, buffer)
            use(i - 1, last)
            out_start(i, buffer, side)

        def two(t, _):
            turn(2 * t + 1, odd, 1, even)

            @pl.when(2 * t + 2 < count)
            def _():
                turn(2 * t + 2, even, 0, odd)

            return 0

        lax.fori_loop(0, count // 2, two, 0)
        ends_even = lax.rem(count, 2) == 1

        @pl.when(ends_even)
        def _():
            use(count - 1, even)

        @pl.when(jnp.logical_not(ends_even))
        def _():
            use(count - 1, odd)

        for leaf in range(per_dev):
            near[:, leaf_slice(leaf)] = total[leaf]
        last_even = jnp.where(ends_even, count - 1, count - 2)
        out_wait(last_even, even, 0)

        @pl.when(count >= 2)
        def _():
            out_wait(jnp.where(ends_even, count - 2, count - 1), odd, 1)

    def near_first(pair, other):
        block_shape = (2, leaf_size, leaf_size)
        return call(
            near_first_body,
            (
                field_shape,
                pltpu.HBM((2 * per_dev, *blocks_shape[1:]), bf16),
                pltpu.HBM((per_dev, *blocks_shape[1:]), bf16),
                shape(couple_shape, bf16),
                shape((leaves * per_dev, cols), f32),
            ),
            [SMEM, SMEM] + [VMEM] * 5,
            (VMEM, HBM, HBM, VMEM, VMEM),
            scratch=[
                pltpu.VMEM(block_shape, bf16),
                pltpu.VMEM(block_shape, bf16),
                pltpu.VMEM((3 * per_dev, leaf_size, 6 * SUB), bf16),
                pltpu.VMEM((per_dev, 6 * SUB, leaf_size), bf16),
                pltpu.VMEM((3 * per_dev, 2 * vec, leaf_size), bf16),
                pltpu.VMEM((per_dev, vec, leaf_size), f32),
                pltpu.SMEM((len(entries) + 1,), jnp.int32),
                pltpu.SemaphoreType.DMA((2,)),
            ],
            flops=10**9,
            limit=NEAR_LIMIT,
        )(near_lists, inter_lists, stacked, pair, other, coarse_points, transfer)

    def near_inner(field, pair, blocks):
        chosen = [entry for entry in entries if entry[0] < 2]
        shape_here = (2 * per_dev, *blocks_shape[1:])

        def body(lists, own, pair, blocks_in, near, blocks, sems):
            def in_copy(block, leaf):
                return pltpu.make_async_copy(
                    blocks_in.at[block, leaf], blocks.at[block, leaf],
                    sems.at[block * per_dev + leaf],
                )

            place = whereabouts()
            hits = [hit(place, lists, *entry) for entry in chosen]
            twice = both_ways(place, lists)
            at = chosen.index(mirrored)
            hits[at] = jnp.logical_and(hits[at], jnp.logical_not(twice))
            for (kind, j, leaf), found in zip(chosen, hits, strict=True):

                @pl.when(found)
                def _():
                    in_copy(kind * per_dev + j, leaf).start()

            near[...] = jnp.zeros_like(near)
            for (kind, j, leaf), found in zip(chosen, hits, strict=True):
                block = kind * per_dev + j

                @pl.when(found)
                def _():
                    in_copy(block, leaf).wait()
                    near[:, leaf_slice(leaf)] += dot3(
                        (own, pair)[kind][:, leaf_slice(j)],
                        blocks[block, leaf, 0],
                        blocks[block, leaf, 1],
                    )

                if (kind, j, leaf) == mirrored:

                    @pl.when(twice)
                    def _():
                        near[:, leaf_slice(0)] += dot3_nt(
                            own[:, leaf_slice(1)], blocks[0, 1, 0], blocks[0, 1, 1]
                        )

        return call(
            body,
            field_shape,
            [SMEM, VMEM, VMEM, HBM],
            VMEM,
            scratch=[pltpu.VMEM(shape_here, bf16), pltpu.SemaphoreType.DMA((len(chosen),))],
            flops=10**8,
            limit=INNER_LIMIT,
        )(near_lists, field, pair, pltpu.with_memory_space_constraint(blocks, pltpu.HBM))

    def near_outer(other, blocks, before):
        def body(lists, other, blocks, before, near):
            near[...] = before[...]
            place = whereabouts()
            for j in range(per_dev):
                for leaf in range(per_dev):

                    @pl.when(hit(place, lists, 2, j, leaf))
                    def _():
                        near[:, leaf_slice(leaf)] += dot3(
                            other[:, leaf_slice(j)], blocks[j, leaf, 0], blocks[j, leaf, 1]
                        )

        return call(
            body,
            field_shape,
            [SMEM, VMEM, VMEM, VMEM],
            VMEM,
            flops=10**8,
            limit=limit,
        )(near_lists, other, blocks, before)

    def halo(field):
        pair = lax.ppermute(field, "leaf", inner)
        other = lax.ppermute(field, "leaf", outer)
        return pair, other

    def build_far(place, marks, received, far):
        group, leaf = place[1], place[0]

        def spots_of(i):
            at = group * leaves + i
            first = received[at, :, piece(pieces)]
            return [first[0:1], first[1:2], received[at, :, piece(pieces + 1)][0:1]]

        mine = spots_of(leaf)
        origin = [x[:, :1] for x in mine]
        scaled = lambda spots: [
            (x - o) * kappa_scale for x, o in zip(spots, origin, strict=True)
        ]
        target = target_factors(scaled(mine))
        for i in range(leaves):
            kernel = matern(source_factors(scaled(spots_of(i))), target)
            for h in range(per_dev):
                m = i * per_dev + h
                at = slice(m * rank, (m + 1) * rank)
                hi, lo = split(kernel[h * rank : (h + 1) * rank] * marks[m : m + 1])
                far[0, at] = hi
                far[1, at] = lo

    far_shape = (2, far_rows + couple_rows, cols)

    def post_body(step, *refs):
        refs = list(refs)
        marks, couple = (refs.pop(0), refs.pop(0)) if step == 1 else (None, None)
        received, interp, near, field = refs[:4]
        refs = refs[4:]
        far, before = (None, None) if step == 1 else (refs.pop(0), refs.pop(0))
        transfer = refs.pop(0) if step < 3 else None
        out, send = refs.pop(0), refs.pop(0)
        place = whereabouts()
        group = place[1]
        if step == 1:
            far, rows = refs.pop(0), refs.pop()
            build_far(place, marks, received, far)
            far[:, far_rows:] = couple[...]
            for i in range(leaves):
                for k in range(pieces):
                    rows[i, 2 * k : 2 * k + 2] = received[group * leaves + i, :, piece(k)]
        else:
            rows = received
        first = 0 if step == 1 else group * leaves
        parts = [rows[first + i] for i in range(leaves)]
        for t in range(1, groups):
            first = lax.rem(group + t, groups) * leaves
            sums = [received[first + i] for i in range(leaves)]
            while len(sums) > 1:
                sums = [sum(sums[i : i + 2]) for i in range(0, len(sums), 2)]
            if step == 1:
                for k in range(pieces):
                    rows[leaves, 2 * k : 2 * k + 2] = sums[0][:, piece(k)]
                parts.append(rows[leaves])
            else:
                parts += sums
        down = dot3(jnp.concatenate(parts, axis=1), far[0], far[1])
        news = []
        for j in range(per_dev):
            here = leaf_slice(j)
            far_part = dot3(down[:, j * rank : (j + 1) * rank], interp[0, j], interp[1, j])
            applied = (near[:, here] + far_part) * (1.0 / (leaf_size * slots))
            term = (applied - centre * field[:vec, here]) * (1.0 / half_width)
            if step > 1:
                term = 2.0 * term - before[:vec, here]
            news.append(term)
            out[:, here] = term
        if step < 3:
            own, up, sems = refs
            copies = Copies(sems)
            coeffs = coefficients(jnp.concatenate(news, axis=1), interp)
            send_all(copies, send, own, up, coeffs, transfer, group)
            copies.finish()
        else:
            squares = None
            for term in news:
                part = jnp.sum(term * term, axis=1, keepdims=True)
                squares = part if squares is None else squares + part
            diagonal = lax.broadcasted_iota(jnp.int32, (vec, 128), 0) == lax.broadcasted_iota(
                jnp.int32, (vec, 128), 1
            )
            row = jnp.sum(jnp.where(diagonal, squares, 0.0), axis=0, keepdims=True)
            for i in range(devices):
                send[i] = row

    def post(step, received, near, field, *rest):
        send_shape = (devices, vec, cols) if step < 3 else (devices, 1, 128)
        outs = [field_shape, shape(send_shape, f32)]
        specs = [VMEM, HBM if step < 3 else VMEM]
        args = [received, interp, near, field, *rest]
        if step == 1:
            outs.append(shape(far_shape, bf16))
            specs.append(VMEM)
            args = [marks, couple, *args]
        scratch = []
        if step < 3:
            args.append(transfer)
            scratch = [
                pltpu.VMEM((vec, cols), f32),
                pltpu.VMEM((vec, cols), f32),
                pltpu.SemaphoreType.DMA((devices,)),
            ]
            if step == 1:
                scratch.append(pltpu.VMEM((leaves + 1, vec, cols), f32))
        return call(
            lambda *refs: post_body(step, *refs),
            tuple(outs),
            [VMEM] * len(args),
            tuple(specs),
            scratch=scratch,
            flops=10**7,
            limit=limit,
        )(*args)

    received = exchange(payload)
    pair, other = halo(stacked)
    near, blocks, other_blocks, couple, marks = near_first(pair, other)

    def again(field):
        pair, other = halo(field)
        near = near_inner(field, pair, blocks)
        return near_outer(other, other_blocks, near)

    term_one, payload, far = post(1, received, near, stacked)
    received = exchange(payload)
    near = again(term_one)
    term_two, payload = post(2, received, near, term_one, far, stacked)
    received = exchange(payload)
    near = again(term_two)
    term_three, payload = post(3, received, near, term_two, far, term_one)
    received = exchange(payload)
    squares = jnp.sum(received, axis=(0, 1))[:vec]
    total_points = width * devices
    return term_three / jnp.sqrt(squares / total_points + 1e-06)[:, None]


def solution(mesh):
    placed = (
        P(None, ("grp", "leaf")),
        P(None, ("grp", "leaf")),
        P(("grp", "leaf"), None),
        P(("grp", "leaf"), None),
        P(("grp", "leaf"), None),
        P(("grp", "leaf"), None, None),
        P(("grp", "leaf"), None, None),
        P(),
    )

    return jax.shard_map(
        on_device, mesh=mesh, in_specs=placed, out_specs=P(None, ("grp", "leaf")), check_vma=False
    )
```
